512 devices in a mesh: seq: 128 (over z, y, core), head: 4 (over x).
Axes of the slice: x: 4, y: 8, z: 8, core: 2. Of those that a mesh axis runs over, the one named last changes fastest.
Arguments:
- queries: bfloat16 [32768, 4096], P('seq', 'head'), may hold values from -6 to 6
- keys: bfloat16 [32768, 512], P(('seq', 'head')), may hold values from -6 to 6
- values: bfloat16 [32768, 512], P(('seq', 'head')), may hold values from -6 to 6
- d_out: bfloat16 [32768, 4096], P('seq', 'head'), may hold values from -6 to 6
- rand_blocks: int32 [512, 8], P('seq'), may hold values from 0 to 511, as said below
- glob_blocks: int32 [2], replicated, may hold values from 0 to 511
Outputs:
- attn_out: bfloat16 [32768, 4096], P('seq', 'head')
- d_queries: bfloat16 [32768, 4096], P('seq', 'head')
- d_keys: bfloat16 [32768, 512], P(('seq', 'head'))
- d_values: bfloat16 [32768, 512], P(('seq', 'head'))
The draws below stay inside these ranges and needn't reach their ends.
Inputs may be any that keep to these rules, and one draw needn't show every extreme that they name: `rand_blocks`: block b lies on index b // 4 of seq. Among the 32 entries of the query blocks of one index of seq, at most 1 name blocks of any one index, and some index of seq reaches 1 for some owner in every draw.
All inputs are finite; a program needn't handle non-finite values.
Results may differ from the reference program's by a relative error of at most 0.012.
Values may be sent and summed in bfloat16 or wider, within the bound.
A program may use at most 64 MiB of HBM per device.

```python
import jax
import jax.numpy as jnp
from jax import lax

DH = 128
QH = 32
KVH = 4
BLOCK = 64
GLOB = 2
RAND = 8
QB_DEV = 4
TOKENS = 32768
NB = 512
N_SEQ = 128


def drawn_pair(key):
    base = jax.random.fold_in(key, 7001)
    first_key, second_key = jax.random.split(base, 2)
    query_mat = jnp.clip(jax.random.normal(first_key, (TOKENS, QH * DH), jnp.float32), -6.0, 6.0)
    key_mat = jnp.clip(jax.random.normal(second_key, (TOKENS, KVH * DH), jnp.float32), -6.0, 6.0)
    return (query_mat, key_mat)


def draw_queries(key, part):
    query_mat, key_mat = drawn_pair(key)
    return query_mat.astype(jnp.bfloat16)


def draw_keys(key, part):
    query_mat, key_mat = drawn_pair(key)
    return key_mat.astype(jnp.bfloat16)


def draw_rand_blocks(key, part):
    base = jax.random.fold_in(key, 9001)
    popular_key, device_key, inner_key = jax.random.split(base, 3)
    capacity = (QB_DEV * RAND + N_SEQ - 1) // N_SEQ
    position_count = N_SEQ * capacity
    wanted = QB_DEV * RAND
    preferred_blocks = (jax.random.randint(popular_key, (N_SEQ,), 0, 8) == 0).astype(jnp.int32)
    position_holder = jnp.arange(position_count, dtype=jnp.int32) // capacity
    extra_score = preferred_blocks[position_holder] * 32768
    random_jitter = jax.random.randint(device_key, (N_SEQ, position_count), 0, 32768)
    sorted_order = (random_jitter + extra_score[None, :]) * position_count + jnp.arange(position_count, dtype=jnp.int32)[None, :]
    ignored, picked = lax.top_k(sorted_order, wanted)
    owners = picked // capacity
    inner = jax.random.randint(inner_key, (N_SEQ, wanted), 0, QB_DEV)
    chosen = owners * QB_DEV + inner
    return chosen.reshape(NB, RAND).astype(jnp.int32)


def steps_of(stream_key, extent, cuts, least, high):
    loudness = 1.0
    for dim, shards_of in cuts:
        steps = jax.random.uniform(jax.random.fold_in(jax.random.fold_in(stream_key, 6), dim), (shards_of,), jnp.float32, least / len(cuts), high / len(cuts))
        loudness = loudness * jnp.repeat(jnp.exp(steps), extent[dim] // shards_of).reshape((-1,) + (1,) * (len(extent) - 1 - dim))
    return loudness


def normal_values(stream_key, dims, scale, bound, cuts=(), held_as=jnp.bfloat16):
    values = scale * jax.random.normal(stream_key, dims, jnp.float32)
    if cuts:
        values = values * steps_of(stream_key, dims, cuts, -0.22, 0.18)
    return jnp.clip(values, -bound, bound).astype(held_as)


def setup_inputs(seed: int = 0) -> dict:
    streams_of = jax.random.split(jax.random.key(seed), 7)
    queries = draw_queries(jax.random.fold_in(streams_of[6], 71), 0)
    keys = draw_keys(jax.random.fold_in(streams_of[6], 71), 0)
    values = normal_values(streams_of[2], (TOKENS, KVH * DH), 1.0, 6.0, ((0, 512),))
    d_out = normal_values(streams_of[3], (TOKENS, QH * DH), 1.0, 6.0, ((0, 128), (1, 4)))
    rand_blocks = draw_rand_blocks(jax.random.fold_in(streams_of[6], 71), 0)
    glob_blocks = jax.random.randint(streams_of[5], (GLOB,), 0, NB).astype(jnp.int32)
    return {"queries": queries, "keys": keys, "values": values, "d_out": d_out, "rand_blocks": rand_blocks, "glob_blocks": glob_blocks}


def reference(queries, keys, values, d_out, rand_blocks, glob_blocks):
    factor = DH ** -0.5
    group = QH // KVH
    count = 3 + GLOB + RAND
    stacked = jnp.concatenate([keys.reshape(NB, BLOCK, KVH, DH), values.reshape(NB, BLOCK, KVH, DH)], axis=3)
    query_all = queries.reshape(NB, BLOCK, KVH, group, DH)
    grad_all = d_out.reshape(NB, BLOCK, KVH, group, DH)
    blocks = jnp.arange(NB, dtype=jnp.int32)
    window = jnp.stack([jnp.maximum(blocks - 1, 0), blocks, jnp.minimum(blocks + 1, NB - 1)], axis=1)
    lists = jnp.concatenate([window, jnp.broadcast_to(glob_blocks[None, :], (NB, GLOB)).astype(jnp.int32), rand_blocks.astype(jnp.int32)], axis=1).astype(jnp.int32)
    valid = jnp.concatenate([(blocks > 0)[:, None], jnp.ones((NB, 1), jnp.bool_), (blocks < NB - 1)[:, None], jnp.ones((NB, GLOB + RAND), jnp.bool_)], axis=1)
    crossing = (window // QB_DEV) != (blocks // QB_DEV)[:, None]
    rounded_flag = jnp.concatenate([crossing, jnp.zeros((NB, GLOB), jnp.bool_), jnp.ones((NB, RAND), jnp.bool_)], axis=1)

    def step(accum, inputs):
        query_block, gradient_tile, spots, allowed, rounding = inputs
        gathered = stacked[spots].astype(jnp.float32).reshape(count * BLOCK, KVH, 2 * DH)
        key_rows = gathered[:, :, :DH]
        value_rows = gathered[:, :, DH:]
        query32 = query_block.astype(jnp.float32)
        grad32 = gradient_tile.astype(jnp.float32)
        scores = jnp.einsum("tkgd,skd->kgts", query32, key_rows) * factor
        columns = jnp.repeat(allowed, BLOCK)
        scores = jnp.where(columns[None, None, None, :], scores, -1.0e30)
        peak = jnp.max(scores, axis=-1, keepdims=True)
        logsum = peak + jnp.log(jnp.sum(jnp.exp(scores - peak), axis=-1, keepdims=True))
        probs = jnp.exp(scores - logsum)
        probs16 = lax.optimization_barrier(probs.astype(jnp.bfloat16)).astype(jnp.float32)
        output = jnp.einsum("kgts,skd->tkgd", probs16, value_rows).astype(jnp.bfloat16)
        delta = jnp.sum(grad32 * output.astype(jnp.float32), axis=-1)
        dprobs = jnp.einsum("tkgd,skd->kgts", grad32, value_rows)
        dscores = probs * (dprobs - jnp.transpose(delta, (1, 2, 0))[..., None])
        dscores16 = lax.optimization_barrier(dscores.astype(jnp.bfloat16)).astype(jnp.float32)
        dquery = (jnp.einsum("kgts,skd->tkgd", dscores16, key_rows) * factor).astype(jnp.bfloat16)
        dkey = jnp.einsum("kgts,tkgd->skd", dscores16, query32) * factor
        dvalue = jnp.einsum("kgts,tkgd->skd", probs16, grad32)
        terms = jnp.concatenate([dkey, dvalue], axis=-1).reshape(count, BLOCK, KVH, 2 * DH)
        shipped = lax.optimization_barrier(terms.astype(jnp.bfloat16)).astype(jnp.float32)
        terms = jnp.where(rounding[:, None, None, None], shipped, terms)
        accum = accum.at[spots].add(terms)
        return accum, (output.reshape(BLOCK, QH * DH), dquery.reshape(BLOCK, QH * DH))

    start = jnp.zeros((NB, BLOCK, KVH, 2 * DH), jnp.float32)
    accum, (outputs, dqueries) = lax.scan(step, start, (query_all, grad_all, lists, valid, rounded_flag))
    d_keys = accum[..., :DH].astype(jnp.bfloat16).reshape(TOKENS, KVH * DH)
    d_values = accum[..., DH:].astype(jnp.bfloat16).reshape(TOKENS, KVH * DH)
    return outputs.reshape(TOKENS, QH * DH), dqueries.reshape(TOKENS, QH * DH), d_keys, d_values
```

```python
import functools

import jax
import jax.numpy as jnp
from jax import lax
from jax.experimental import pallas as pl
from jax.experimental.pallas import tpu as pltpu
from jax.sharding import PartitionSpec as P

DH = 128
KVH = 4
HEADS = 8
BLOCK = 64
RAND = 8
PAIR = 2 * DH
RING = 8
NEG_FILL = -1e30
BF16 = jnp.bfloat16
F32 = jnp.float32
MESH = pl.DeviceIdType.MESH

ORDER = (0, 1, -1, 2, -2, 3, -3, 4)
SLOT = {d: i for i, d in enumerate(ORDER)}
UNITS = ((0, 1), (1, 3), (3, 5), (5, 7), (7, 8))
UNIT_OF = {d: u for u, (lo, hi) in enumerate(UNITS) for d in ORDER[lo:hi]}
FAR = {1: (0, 1, 4), -1: (2, 3)}
GROUPS = ((0, 3), (3, 7), (7, 8))
CHUNK_US = 1.41
PARTNER_US = 0.25
HOP_US = 1.7
ROWS = 40
NONE_ROW = 36


def axis_of(half, major):
    return "zy"[half] if major else "yz"[half]


def ordered(tasks):
    arrival, free, result = {}, {}, []
    waiting = list(tasks)
    while waiting:
        best = None
        for task in waiting:
            if all(dep in arrival for dep in task[3]):
                ready = max([arrival[dep] for dep in task[3]], default=0.0)
                if best is None or ready < best[0]:
                    best = (ready, task)
        ready, task = best
        waiting.remove(task)
        name, link, time, deps = task
        end = max(ready, free.get(link, 0.0)) + time
        free[link] = end
        arrival[name] = end + HOP_US
        result.append(task)
    return result, max(arrival.values())


def gather_tasks():
    tasks = []
    delivered = {}
    for half in (0, 1):
        minor, major = axis_of(half, False), axis_of(half, True)
        for sign, ends in ((1, (0, 1, 2, 3)), (-1, (0, -1, -2))):
            for d in ends:
                name = ("m", half, sign, d)
                deps = () if d == 0 else (("m", half, sign, d - sign),)
                tasks.append((name, (minor, sign), CHUNK_US, deps))
                delivered[half, 0, SLOT[d + sign]] = name
        for sign in (1, -1):
            for step in range(4):
                for u, (lo, hi) in enumerate(UNITS):
                    d = step * sign
                    if step == 3 and u not in FAR[sign]:
                        continue
                    name = ("M", half, sign, d, u)
                    if d == 0:
                        deps = tuple(delivered[half, 0, s] for s in range(lo, hi) if s)
                    else:
                        deps = (("M", half, sign, d - sign, u),)
                    tasks.append((name, (major, sign), CHUNK_US * (hi - lo), deps))
                    to = 7 if step == 3 else SLOT[d + sign]
                    for s in range(lo, hi):
                        delivered[half, to, s] = name
        for row in range(RING):
            for lo, hi in GROUPS:
                deps = tuple(
                    dict.fromkeys(delivered[half, row, s] for s in range(lo, hi) if row or s)
                )
                tasks.append((("P", half, row, lo, hi), "p", PARTNER_US * (hi - lo), deps))
    return ordered(tasks)[0]


def scatter_tasks():
    tasks = []
    for half in (0, 1):
        minor, major = axis_of(half, False), axis_of(half, True)
        for step in (4, 3, 2, 1):
            for u in (4, 3, 2, 1, 0):
                for sign in (1, -1):
                    lo, hi = UNITS[u]
                    far = u in FAR[sign]
                    if step == 4 and not far:
                        continue
                    name = ("M", half, sign, step, u)
                    deps = ()
                    if step < 3 or (step == 3 and far):
                        deps = (("M", half, sign, step + 1, u),)
                    tasks.append((name, (major, sign), CHUNK_US * (hi - lo), deps))
        for sign, top in ((1, 4), (-1, 3)):
            for step in range(top, 0, -1):
                u = UNIT_OF[step * sign]
                deps = (("M", half, 1, 1, u), ("M", half, -1, 1, u))
                if step < top:
                    deps += (("m", half, sign, step + 1),)
                tasks.append((("m", half, sign, step), (minor, sign), CHUNK_US, deps))
        deps = (("M", half, 1, 1, 0), ("M", half, -1, 1, 0), ("m", half, 1, 1), ("m", half, -1, 1))
        tasks.append((("F", half), ("f", half), 0.0, deps))
    return ordered(tasks)[0]


GATHER = gather_tasks()
SCATTER = scatter_tasks()
GATHER_SENDS = {task[0]: i for i, task in enumerate(GATHER)}
SCATTER_SENDS = {t[0]: i for i, t in enumerate(t for t in SCATTER if t[0][0] != "F")}


def place():
    seq = lax.axis_index("seq")
    head = lax.axis_index("head")
    return seq, head, seq // 16, (seq // 2) % RING, seq % 2


def neighbours(seq, head, z, y, core):
    up = lambda v: lax.rem(v + 1, RING)
    down = lambda v: lax.rem(v + RING - 1, RING)
    index = lambda zz, yy, cc: zz * 16 + yy * 2 + cc
    peers = {
        ("z", 1): index(up(z), y, core),
        ("z", -1): index(down(z), y, core),
        ("y", 1): index(z, up(y), core),
        ("y", -1): index(z, down(y), core),
        "p": index(z, y, 1 - core),
    }
    return {k: {"seq": v, "head": head} for k, v in peers.items()}


def enter(peers, seq, head):
    barrier = pltpu.get_barrier_semaphore()
    everyone = list(peers.values())
    everyone += [{"seq": seq, "head": lax.rem(head + j, KVH)} for j in (1, 2, 3)]
    for peer in everyone:
        pl.semaphore_signal(barrier, inc=1, device_id=peer, device_id_type=MESH)
    pl.semaphore_wait(barrier, len(everyone))


def remote(src, dst, send, recv, peer):
    return pltpu.make_async_remote_copy(
        src_ref=src,
        dst_ref=dst,
        send_sem=send,
        recv_sem=recv,
        device_id=peer,
        device_id_type=MESH,
    )


def gather_kernel(keys, values, rand, out, rand_out, send, recv, xsend, xrecv, isem, lsem):
    seq, head, z, y, core = place()
    peers = neighbours(seq, head, z, y, core)
    enter(peers, seq, head)
    pieces = ((keys, 0), (values, DH))
    copies = []
    for j in (1, 2, 3):
        to = lax.rem(head + j, KVH)
        for n, (source, lane) in enumerate(pieces):
            copies.append(
                remote(
                    source.at[:, pl.ds(pl.multiple_of(to * DH, DH), DH)],
                    out.at[0, head // 2, 0, lax.rem(head, 2), :, pl.ds(lane, DH)],
                    xsend.at[j - 1, n],
                    xrecv.at[j - 1, n],
                    {"seq": seq, "head": to},
                )
            )
            copies[-1].start()
    index_copy = remote(rand, rand_out, isem.at[0], isem.at[1], peers["p"])
    index_copy.start()
    local = []
    for n, (source, lane) in enumerate(pieces):
        local.append(
            pltpu.make_async_copy(
                source.at[:, pl.ds(pl.multiple_of(head * DH, DH), DH)],
                out.at[0, head // 2, 0, lax.rem(head, 2), :, pl.ds(lane, DH)],
                lsem.at[n],
            )
        )
        local[-1].start()
    for copy in local:
        copy.wait()
    for copy in copies:
        copy.wait_recv()

    started = {}
    waited = set()
    for name, link, _, deps in GATHER:
        for dep in deps:
            if dep not in waited:
                waited.add(dep)
                started[dep].wait_recv()
        half = name[1]
        if name[0] == "m":
            _, _, sign, d = name
            src = out.at[0, half, 0, pl.ds(2 * SLOT[d], 2)]
            dst = out.at[0, half, 0, pl.ds(2 * SLOT[d + sign], 2)]
        elif name[0] == "M":
            _, _, sign, d, u = name
            lo, hi = UNITS[u]
            to = 7 if abs(d) == 3 else SLOT[d + sign]
            src = out.at[0, half, SLOT[d], pl.ds(2 * lo, 2 * (hi - lo))]
            dst = out.at[0, half, to, pl.ds(2 * lo, 2 * (hi - lo))]
        else:
            _, _, row, lo, hi = name
            src = out.at[0, half, row, pl.ds(2 * lo, 2 * (hi - lo))]
            dst = out.at[1, half, row, pl.ds(2 * lo, 2 * (hi - lo))]
        i = GATHER_SENDS[name]
        copy = remote(src, dst, send.at[i], recv.at[i], peers[link])
        copy.start()
        started[name] = copy
    for name, copy in started.items():
        if name not in waited:
            copy.wait_recv()
    for copy in copies:
        copy.wait_send()
    for copy in started.values():
        copy.wait_send()
    index_copy.wait()


def gather_all(keys, values, rand):
    count = len(GATHER)
    return pl.pallas_call(
        gather_kernel,
        out_shape=(
            jax.ShapeDtypeStruct((2, 2, RING, 2 * RING, BLOCK, PAIR), BF16),
            jax.ShapeDtypeStruct(rand.shape, jnp.int32),
        ),
        in_specs=[pl.BlockSpec(memory_space=pltpu.VMEM)] * 3,
        out_specs=(pl.BlockSpec(memory_space=pl.ANY), pl.BlockSpec(memory_space=pltpu.VMEM)),
        scratch_shapes=[
            pltpu.SemaphoreType.DMA((count,)),
            pltpu.SemaphoreType.DMA((count,)),
            pltpu.SemaphoreType.DMA((3, 2)),
            pltpu.SemaphoreType.DMA((3, 2)),
            pltpu.SemaphoreType.DMA((2,)),
            pltpu.SemaphoreType.DMA((2,)),
        ],
        compiler_params=pltpu.CompilerParams(collective_id=1, has_side_effects=True),
        name="gather_blocks",
    )(keys, values, rand)


def scatter_kernel(
    index, table, own, dk, dv, far, mirror, zero, line, start, final, send, recv, xsend, xrecv, psem, lsem
):
    seq, head, z, y, core = place()
    peers = neighbours(seq, head, z, y, core)
    enter(peers, seq, head)
    partner = remote(table, mirror, psem.at[0], psem.at[1], peers["p"])
    partner.start()
    partner.wait_recv()

    def local_sum(spot):
        total = table[index[0, spot]].astype(F32) + table[index[1, spot]].astype(F32)
        return total + (mirror[index[2, spot]].astype(F32) + mirror[index[3, spot]].astype(F32))

    started = {}
    waited = set()
    for name, link, _, deps in SCATTER:
        for dep in deps:
            if dep not in waited:
                waited.add(dep)
                started[dep].wait_recv()
        half = name[1]
        if name[0] == "F":

            @pl.loop(0, 2)
            def _(j):
                total = local_sum(half * 128 + j) + own[half * 2 + j]
                total += far[half, 0, j].astype(F32) + zero[half, j].astype(F32)
                total += line[half, j].astype(F32) + start[half, j].astype(F32)
                final[half * 2 + j] = total.astype(BF16)

            continue
        if name[0] == "M":
            _, _, sign, step, u = name
            lo, hi = UNITS[u]
            row = SLOT[step * sign] if step < 4 else 7
            arrived = bool(deps)

            @pl.loop(0, 2 * (hi - lo))
            def _(j):
                j = 2 * lo + j
                total = local_sum((half * 8 + row) * 16 + j)
                if arrived:
                    total += far[half, row, j].astype(F32)
                far[half, row, j] = total.astype(BF16)

            size = pl.ds(2 * lo, 2 * (hi - lo))
            src = far.at[half, row, size]
            if step > 1:
                dst = far.at[half, SLOT[(step - 1) * sign], size]
            elif sign > 0:
                dst = far.at[half, 0, size]
            else:
                dst = zero.at[half, size]
        else:
            _, _, sign, step = name
            at = 2 * SLOT[step * sign]
            arrived = len(deps) > 2

            @pl.loop(0, 2)
            def _(j):
                j = at + j
                total = local_sum(half * 128 + j)
                total += far[half, 0, j].astype(F32) + zero[half, j].astype(F32)
                if arrived:
                    total += line[half, j].astype(F32)
                line[half, j] = total.astype(BF16)

            src = line.at[half, pl.ds(at, 2)]
            if step > 1:
                dst = line.at[half, pl.ds(2 * SLOT[(step - 1) * sign], 2)]
            elif sign > 0:
                dst = line.at[half, pl.ds(0, 2)]
            else:
                dst = start.at[half]
        i = SCATTER_SENDS[name]
        copy = remote(src, dst, send.at[i], recv.at[i], peers[link[0], -link[1]])
        copy.start()
        started[name] = copy

    pieces = ((dk, 0), (dv, DH))
    here = pl.ds(pl.multiple_of(head * DH, DH), DH)
    copies = []
    for j in (1, 2, 3):
        to = lax.rem(head + j, KVH)
        for n, (target, lane) in enumerate(pieces):
            copies.append(
                remote(
                    final.at[to, :, pl.ds(lane, DH)],
                    target.at[:, here],
                    xsend.at[j - 1, n],
                    xrecv.at[j - 1, n],
                    {"seq": seq, "head": to},
                )
            )
            copies[-1].start()
    local = []
    for n, (target, lane) in enumerate(pieces):
        local.append(
            pltpu.make_async_copy(final.at[head, :, pl.ds(lane, DH)], target.at[:, here], lsem.at[n])
        )
        local[-1].start()
    for copy in local + copies:
        copy.wait()
    partner.wait_send()
    for copy in started.values():
        copy.wait_send()


def scatter_all(index, table, own):
    count = len(SCATTER_SENDS)
    return pl.pallas_call(
        scatter_kernel,
        out_shape=(jax.ShapeDtypeStruct((BLOCK, KVH * DH), BF16),) * 2,
        in_specs=[
            pl.BlockSpec(memory_space=pltpu.SMEM),
            pl.BlockSpec(memory_space=pltpu.VMEM),
            pl.BlockSpec(memory_space=pltpu.VMEM),
        ],
        out_specs=(pl.BlockSpec(memory_space=pl.ANY),) * 2,
        scratch_shapes=[
            pltpu.VMEM((2, RING, 2 * RING, BLOCK, PAIR), BF16),
            pltpu.VMEM((ROWS, BLOCK, PAIR), BF16),
            pltpu.VMEM((2, 2 * RING, BLOCK, PAIR), BF16),
            pltpu.VMEM((2, 2 * RING, BLOCK, PAIR), BF16),
            pltpu.VMEM((2, 2, BLOCK, PAIR), BF16),
            pltpu.VMEM((4, BLOCK, PAIR), BF16),
            pltpu.SemaphoreType.DMA((count,)),
            pltpu.SemaphoreType.DMA((count,)),
            pltpu.SemaphoreType.DMA((3, 2)),
            pltpu.SemaphoreType.DMA((3, 2)),
            pltpu.SemaphoreType.DMA((2,)),
            pltpu.SemaphoreType.DMA((2,)),
        ],
        compiler_params=pltpu.CompilerParams(collective_id=2, has_side_effects=True),
        name="scatter_terms",
    )(index, table, own)


def attention_kernel(spots, edges, same, queries, d_out, library, out, dq, table, own, kv, near, glob, sems):
    copies = [
        pltpu.make_async_copy(library.at[spots[e]], kv.at[e], sems.at[e]) for e in range(ROWS)
    ]
    for copy in copies:
        copy.start()
    near[...] = jnp.zeros_like(near)
    glob[...] = jnp.zeros_like(glob)
    table[NONE_ROW:] = jnp.zeros((ROWS - NONE_ROW, BLOCK, PAIR), BF16)
    for copy in copies:
        copy.wait()
    factor = DH ** (-0.5)
    dims = lambda a, b: (((a,), (b,)), ((), ()))

    def dot(a, b, at, bt):
        return lax.dot_general(a, b, dims(at, bt), preferred_element_type=F32)

    @pl.loop(0, 4)
    def _(i):
        rows = pl.ds(pl.multiple_of(i * BLOCK, BLOCK), BLOCK)
        stack = lambda ref: jnp.concatenate(
            [ref[rows, h * DH : (h + 1) * DH] for h in range(HEADS)], axis=0
        )
        q, g = stack(queries), stack(d_out)
        pairs = jnp.concatenate(
            [
                kv[pl.ds(i, 3)].reshape(3 * BLOCK, PAIR),
                kv[6:8].reshape(2 * BLOCK, PAIR),
                kv[pl.ds(8 + i * RAND, RAND)].reshape(RAND * BLOCK, PAIR),
            ],
            axis=0,
        )
        k, v = pairs[:, :DH], pairs[:, DH:]
        scores = dot(k, q, 1, 1) * factor
        cut_first = jnp.logical_and(i == 0, edges[0] == 1)
        cut_last = jnp.logical_and(i == 3, edges[1] == 1)
        scores = jnp.concatenate(
            [
                jnp.where(cut_first, NEG_FILL, scores[:BLOCK]),
                scores[BLOCK : 2 * BLOCK],
                jnp.where(cut_last, NEG_FILL, scores[2 * BLOCK : 3 * BLOCK]),
                scores[3 * BLOCK :],
            ],
            axis=0,
        )
        peak = jnp.max(scores, axis=0, keepdims=True)
        weights = jnp.exp(scores - peak)
        probs = weights * (1.0 / jnp.sum(weights, axis=0, keepdims=True))
        probs16 = probs.astype(BF16)
        result = dot(v, probs16, 0, 0).astype(BF16)
        delta = jnp.sum(g.T.astype(F32) * result.astype(F32), axis=0, keepdims=True)
        dprobs = dot(v, g, 1, 1)
        dscores = (probs * (dprobs - delta)).astype(BF16)
        dquery = (dot(k, dscores, 0, 0) * factor).astype(BF16).T
        result = result.T
        for h in range(HEADS):
            out[rows, h * DH : (h + 1) * DH] = result[h * BLOCK : (h + 1) * BLOCK]
            dq[rows, h * DH : (h + 1) * DH] = dquery[h * BLOCK : (h + 1) * BLOCK]
        dkey = dot(dscores, q, 1, 0) * factor
        dvalue = dot(probs16, g, 1, 0)
        terms = jnp.concatenate([dkey, dvalue], axis=1)
        near[pl.ds(i, 3)] += terms[: 3 * BLOCK].reshape(3, BLOCK, PAIR)
        glob[...] += terms[3 * BLOCK : 5 * BLOCK].reshape(2, BLOCK, PAIR)
        table[pl.ds(i * RAND, RAND)] = terms[5 * BLOCK :].astype(BF16).reshape(RAND, BLOCK, PAIR)

    own[...] = near[1:5]
    rest = (
        near[0].astype(BF16).astype(F32),
        near[5].astype(BF16).astype(F32),
        glob[0],
        glob[1],
    )
    for a in range(4):
        total = rest[a]
        for b in range(4):
            if a != b:
                total += jnp.where(same[a, b] == 1, rest[b], 0.0)
        table[32 + a] = total.astype(BF16)


def attention(spots, edges, same, queries, d_out, library):
    smem = pl.BlockSpec(memory_space=pltpu.SMEM)
    vmem = pl.BlockSpec(memory_space=pltpu.VMEM)
    return pl.pallas_call(
        attention_kernel,
        out_shape=(
            jax.ShapeDtypeStruct(queries.shape, BF16),
            jax.ShapeDtypeStruct(queries.shape, BF16),
            jax.ShapeDtypeStruct((ROWS, BLOCK, PAIR), BF16),
            jax.ShapeDtypeStruct((4, BLOCK, PAIR), F32),
        ),
        in_specs=[smem, smem, smem, vmem, vmem, pl.BlockSpec(memory_space=pl.ANY)],
        out_specs=(vmem,) * 4,
        scratch_shapes=[
            pltpu.VMEM((ROWS, BLOCK, PAIR), BF16),
            pltpu.VMEM((6, BLOCK, PAIR), F32),
            pltpu.VMEM((2, BLOCK, PAIR), F32),
            pltpu.SemaphoreType.DMA((ROWS,)),
        ],
        compiler_params=pltpu.CompilerParams(vmem_limit_bytes=60 * 1024 * 1024),
        name="block_attention",
    )(spots, edges, same, queries, d_out, library)


def slot_of(d):
    d = d % RING
    return jnp.where(d == 0, 0, jnp.where(d <= 4, 2 * d - 1, 2 * (RING - d)))


def body(queries, keys, values, d_out, rand_blocks, glob_blocks):
    seq, head, z, y, core = place()
    library, partner_rand = gather_all(keys, values, rand_blocks)
    library = library.reshape(512, BLOCK, PAIR)
    seq_count = lax.axis_size("seq")

    first = seq * 4
    window = jnp.clip(first - 1 + jnp.arange(6, dtype=jnp.int32), 0, seq_count * 4 - 1)
    ids = jnp.concatenate([window, glob_blocks, rand_blocks.reshape(-1)])
    owner, inner = ids // 4, ids % 4
    dz = slot_of(z - owner // 16)
    dy = slot_of(y - (owner // 2) % RING)
    half = inner // 2
    other = (owner % 2 != core).astype(jnp.int32)
    major = jnp.where(half == 0, dz, dy)
    minor = jnp.where(half == 0, dy, dz)
    spots = (((other * 2 + half) * 8 + major) * 8 + minor) * 2 + inner % 2
    edges = jnp.stack([seq == 0, seq == seq_count - 1]).astype(jnp.int32)

    def entries(at):
        return jnp.concatenate([jnp.stack([at * 4 - 1, at * 4 + 4]), glob_blocks])

    mine = entries(seq)
    same = (mine[:, None] == mine[None, :]).astype(jnp.int32)
    out, dq, table, own = attention(spots, edges, same, queries, d_out, library)

    flat = jnp.arange(256, dtype=jnp.int32)
    half = flat // 128

    def offset(slot):
        return jnp.where(slot % 2 == 1, (slot + 1) // 2, -(slot // 2))

    far, near = offset((flat // 16) % 8), offset((flat // 2) % 8)
    oz = (z - jnp.where(half == 0, far, near)) % RING
    oy = (y - jnp.where(half == 0, near, far)) % RING
    block = (oz * 16 + oy * 2 + core) * 4 + half * 2 + flat % 2

    def lookup(ids, base):
        numbers = base + jnp.arange(ids.shape[0], dtype=jnp.int32)
        hits = jnp.where(block[None, :] == ids[:, None], numbers[:, None], NONE_ROW)
        return jnp.min(hits, axis=0)

    index = jnp.stack(
        [
            lookup(rand_blocks.reshape(-1), 0),
            lookup(mine, 32),
            lookup(partner_rand.reshape(-1), 0),
            lookup(entries(seq + 1 - 2 * core), 32),
        ]
    )
    dk, dv = scatter_all(index, table, own)
    return (out, dq, dk, dv)


def solution(mesh):
    in_specs = (
        P("seq", "head"),
        P(("seq", "head"), None),
        P(("seq", "head"), None),
        P("seq", "head"),
        P("seq", None),
        P(),
    )
    out_specs = (
        P("seq", "head"),
        P("seq", "head"),
        P(("seq", "head"), None),
        P(("seq", "head"), None),
    )
    return jax.shard_map(body, mesh=mesh, in_specs=in_specs, out_specs=out_specs, check_vma=False)
```

```python
import jax
import jax.numpy as jnp
from jax import lax
from jax.experimental import pallas as pl
from jax.experimental.pallas import tpu as pltpu
from jax.sharding import PartitionSpec as P

DH = 128
KVH = 4
HEADS = 8
BLOCK = 64
RAND = 8
PAIR = 2 * DH
RING = 8
NEG_FILL = -1e30
BF16 = jnp.bfloat16
F32 = jnp.float32
MESH = pl.DeviceIdType.MESH

ORDER = (0, 1, -1, 2, -2, 3, -3, 4)
SLOT = {d: i for i, d in enumerate(ORDER)}
ROWS = (0, 3, -3, 1, -1, 2, -2, 4)
PATH = {1: 24, -1: 25, 2: 26, -2: 27}
CHUNKS = 28
INNER = ((1, 3), (3, 5), (5, 7), (7, 8))
LEAVES = (
    (1, 1, 7, ((0, 3), (7, 8))),
    (2, -1, 7, ((3, 5), (5, 7))),
    (1, -1, 5, INNER),
    (2, 1, 6, INNER),
    (0, 1, 3, INNER),
    (0, -1, 4, INNER),
)
SIDES = {("z", 1): 0, ("z", -1): 1, ("y", 1): 2, ("y", -1): 3}
CHUNK_US = 1.78
HALF_US = 0.05
HOP_US = 1.7
KV_ROWS = 40
TERMS = 36
NO_TERM = 34


def axis_of(half, major):
    return "zy"[half] if major else "yz"[half]


def ordered(tasks):
    arrival, free, result = {}, {}, []
    waiting = list(tasks)
    while waiting:
        best = None
        for task in waiting:
            if all(dep in arrival for dep in task[3]):
                ready = max([arrival[dep] for dep in task[3]], default=0.0)
                if best is None or ready < best[0]:
                    best = (ready, task)
        ready, task = best
        waiting.remove(task)
        name, link, time, deps = task
        end = max(ready, free.get(link, 0.0)) + time
        free[link] = end
        arrival[name] = end + HOP_US
        result.append(task)
    return result, max(arrival.values())


def far_sign(half, row):
    return 1 if (half + row) % 2 == 0 else -1


def gather_tasks():
    tasks = []
    for half in (0, 1):
        minor, major = axis_of(half, False), axis_of(half, True)
        whole, leaf = {}, {}
        for step in range(3):
            for sign in (1, -1):
                name = ("H", half, sign, step)
                deps = (("H", half, sign, step - 1),) if step else ()
                tasks.append((name, (major, sign), CHUNK_US, deps))
                if step < 2:
                    whole[PATH[sign * (step + 1)]] = name
                else:
                    whole[8 if sign > 0 else 16] = name
        for row in range(3):
            far = far_sign(half, row)
            for sign in (1, -1):
                for step in range(4 if sign == far else 3):
                    name = ("m", half, row, sign, step)
                    if step:
                        deps = (("m", half, row, sign, step - 1),)
                    else:
                        deps = (whole[8 * row],) if row else ()
                    tasks.append((name, (minor, sign), CHUNK_US, deps))
                    to = 7 if step == 3 else SLOT[sign * (step + 1)]
                    whole[8 * row + to] = name
        for row, sign, to, ranges in LEAVES:
            for lo, hi in ranges:
                name = ("L", half, row, sign, to, lo, hi)
                deps = tuple(whole[8 * row + s] for s in range(lo, hi) if row or s)
                tasks.append((name, (major, sign), CHUNK_US * (hi - lo) / 2, deps))
                for s in range(lo, hi):
                    leaf[to, s] = name
        copies = tuple(whole.values())
        for sign in (1, -1):
            tasks.append((("G", half, sign), (major, sign), CHUNK_US / 2, copies))
        for sign in (1, -1):
            tasks.append((("X", half, sign), "p", HALF_US, (("G", half, sign),)))
        for row in range(8):
            groups = ((0, 5), (5, 8)) if row < 7 else ((0, 3), (3, 7), (7, 8))
            for lo, hi in groups:
                deps = []
                for s in range(lo, hi):
                    if row < 3:
                        deps.append(whole.get(8 * row + s))
                    elif row < 7 and s == 0:
                        deps.append(whole[PATH[ROWS[row]]])
                    else:
                        deps.append(leaf[row, s])
                deps = tuple(dict.fromkeys(d for d in deps if d))
                tasks.append((("P", half, row, lo, hi), "p", HALF_US * (hi - lo), deps))
    return ordered(tasks)[0]


def children(row, slot):
    if row == 0:
        return [(3, 1), (4, -1)] if slot else []
    result = []
    if slot:
        result.append((5, -1) if row == 1 else (6, 1))
    if row == 1 and slot in (0, 1, 2, 7):
        result.append((7, 1))
    if row == 2 and slot in (3, 4, 5, 6):
        result.append((7, -1))
    return result


def scatter_tasks():
    tasks = []
    for half in (0, 1):
        major = axis_of(half, True)
        for sign in (1, -1):
            tasks.append((("G", half, sign), (major, sign), CHUNK_US / 2, ()))
    leaf = {}
    for row, sign, to, ranges in LEAVES:
        for lo, hi in reversed(ranges):
            for half in (0, 1):
                major = axis_of(half, True)
                name = ("L", half, to, sign, lo, hi)
                tasks.append((name, (major, -sign), CHUNK_US * (hi - lo) / 2, ()))
                for s in range(lo, hi):
                    leaf[half, to, s] = name
    for half in (0, 1):
        minor, major = axis_of(half, False), axis_of(half, True)
        extra = (("G", half, 1), ("G", half, -1))

        def leaves(row, slot):
            return tuple(leaf[half, to, slot] for to, _ in children(row, slot)) + extra

        for row in (1, 2, 0):
            for sign in (1, -1):
                top = 4 if sign == far_sign(half, row) else 3
                for step in range(top, 0, -1):
                    deps = leaves(row, 7 if step == 4 else SLOT[sign * step])
                    if step < top:
                        deps += (("m", half, row, sign, step + 1),)
                    tasks.append((("m", half, row, sign, step), (minor, -sign), CHUNK_US, deps))
        for sign in (1, -1):
            row = 1 if sign > 0 else 2
            for step in (3, 2, 1):
                if step == 3:
                    deps = leaves(row, 0) + (("m", half, row, 1, 1), ("m", half, row, -1, 1))
                else:
                    deps = (("H", half, sign, step + 1),)
                tasks.append((("H", half, sign, step), (major, -sign), CHUNK_US, deps))
        deps = tuple((k, half, s, 1) for k in "H" for s in (1, -1))
        deps += (("m", half, 0, 1, 1), ("m", half, 0, -1, 1))
        tasks.append((("F", half), ("f", half), 0.0, deps))
    return ordered(tasks)[0]


GATHER = gather_tasks()
SCATTER = scatter_tasks()
GATHER_SENDS = {task[0]: i for i, task in enumerate(GATHER)}
SCATTER_SENDS = {t[0]: i for i, t in enumerate(t for t in SCATTER if t[0][0] != "F")}


def place():
    seq = lax.axis_index("seq")
    head = lax.axis_index("head")
    return seq, head, seq // 16, (seq // 2) % RING, seq % 2


def neighbours(seq, head, z, y, core):
    up = lambda v: lax.rem(v + 1, RING)
    down = lambda v: lax.rem(v + RING - 1, RING)
    index = lambda zz, yy, cc: zz * 16 + yy * 2 + cc
    count = 2 * RING * RING
    peers = {}
    for name, cc in ((0, core), (1, 1 - core)):
        peers["z", 1, name] = index(up(z), y, cc)
        peers["z", -1, name] = index(down(z), y, cc)
        peers["y", 1, name] = index(z, up(y), cc)
        peers["y", -1, name] = index(z, down(y), cc)
    peers["p"] = index(z, y, 1 - core)
    peers["next"] = lax.rem(seq + 1, count)
    peers["last"] = lax.rem(seq + count - 1, count)
    return {k: {"seq": v, "head": head} for k, v in peers.items()}


def enter(peers, seq, head):
    barrier = pltpu.get_barrier_semaphore()
    everyone = list(peers.values())
    everyone += [{"seq": seq, "head": lax.rem(head + j, KVH)} for j in (1, 2, 3)]
    for peer in everyone:
        pl.semaphore_signal(barrier, inc=1, device_id=peer, device_id_type=MESH)
    pl.semaphore_wait(barrier, len(everyone))


def remote(src, dst, send, recv, peer):
    return pltpu.make_async_remote_copy(
        src_ref=src,
        dst_ref=dst,
        send_sem=send,
        recv_sem=recv,
        device_id=peer,
        device_id_type=MESH,
    )


def owner_of(half, z, y, core, far, near):
    dz, dy = (far, near) if half == 0 else (near, far)
    return lax.rem(z - dz + RING, RING) * 16 + lax.rem(y - dy + RING, RING) * 2 + core


def chunk_offsets(chunk):
    if chunk < 24:
        return ROWS[chunk // 8], ORDER[chunk % 8]
    return (1, -1, 2, -2)[chunk - 24], 0


def gather_kernel(
    keys, values, rand, want, glob, sel_out, near_out, cand_out, rand_out, wants,
    full0, full1, picked, staged, extra, scal, send, recv, xsend, xrecv, osend, orecv, lsem, csem,
):
    seq, head, z, y, core = place()
    peers = neighbours(seq, head, z, y, core)
    full = (full0, full1)
    enter(peers, seq, head)
    pieces = (keys, values)
    xcopies = []
    for j in (1, 2, 3):
        to = lax.rem(head + j, KVH)
        for n, source in enumerate(pieces):
            xcopies.append(
                remote(
                    source.at[:, pl.ds(pl.multiple_of(to * DH, DH), DH)],
                    full[n].at[0, head],
                    xsend.at[j - 1, n],
                    xrecv.at[j - 1, n],
                    {"seq": seq, "head": to},
                )
            )
            xcopies[-1].start()
    ocopies = [remote(want, wants.at[9], osend.at[0], orecv.at[0], peers["p"])]
    for (axis, sign), side in SIDES.items():
        back = SIDES[axis, -sign] * 2
        for r in (0, 1):
            i = len(ocopies)
            peer = peers[axis, sign, r]
            ocopies.append(remote(want, wants.at[back + r], osend.at[i], orecv.at[i], peer))
    ocopies.append(remote(rand, rand_out, osend.at[9], orecv.at[9], peers["p"]))
    for copy in ocopies:
        copy.start()
    local = [pltpu.make_async_copy(want, wants.at[8], lsem.at[0])]
    for n, source in enumerate(pieces):
        mine = source.at[:, pl.ds(pl.multiple_of(head * DH, DH), DH)]
        local.append(pltpu.make_async_copy(mine, full[n].at[0, head], lsem.at[1 + n]))
    for copy in local:
        copy.start()
    for copy in local:
        copy.wait()
    for copy in xcopies:
        copy.wait_recv()

    started = {}
    waited = set()
    tail = []

    def wait_for(deps):
        for dep in deps:
            if dep not in waited:
                waited.add(dep)
                started[dep].wait_recv()

    def finish_start():
        for copy in ocopies:
            copy.wait_recv()
        scalars = pltpu.make_async_copy(wants, scal, lsem.at[0])
        scalars.start()
        for half in (0, 1):
            i = 10 + 2 * half
            tail.append(remote(full[half].at[0, 3], near_out.at[half, 0], osend.at[i], orecv.at[i], peers["next"]))
            tail.append(
                remote(full[half].at[0, 0], near_out.at[half, 5], osend.at[i + 1], orecv.at[i + 1], peers["last"])
            )
            tail.append(
                pltpu.make_async_copy(full[half].at[0], near_out.at[half, pl.ds(1, 4)], lsem.at[1 + half])
            )
        for copy in tail:
            copy.start()
        scalars.wait()

    def pick(half, chunk, side):
        far, near = chunk_offsets(chunk)
        inner = scal[side, 0, owner_of(half, z, y, core, far, near)]
        block = full[half][chunk, 0]
        for b in (1, 2, 3):
            block = jnp.where(inner == b, full[half][chunk, b], block)
        return block

    ready = False
    locals_ = []
    for name, link, _, deps in GATHER:
        wait_for(deps)
        kind, half = name[:2]
        major = axis_of(half, True)
        if kind in "LP" and not ready:
            finish_start()
            ready = True
        i = GATHER_SENDS[name]
        peer = peers["p"] if link == "p" else peers[link[0], link[1], 0]
        extra_sends = []
        if kind == "H":
            _, _, sign, step = name
            src = full[half].at[PATH[sign * step] if step else 0]
            dst = full[half].at[PATH[sign * (step + 1)] if step < 2 else (8 if sign > 0 else 16)]
        elif kind == "m":
            _, _, row, sign, step = name
            src = full[half].at[8 * row + SLOT[sign * step]]
            dst = full[half].at[8 * row + (7 if step == 3 else SLOT[sign * (step + 1)])]
        elif kind == "L":
            _, _, row, sign, to, lo, hi = name
            side = SIDES[major, sign] * 2
            for s in range(lo, hi):
                for r in (0, 1):
                    staged[half, r, to, s] = pick(half, 8 * row + s, side + r)
            src = staged.at[half, :, to, pl.ds(lo, hi - lo)]
            dst = picked.at[half, :, to, pl.ds(lo, hi - lo)]
        elif kind == "P":
            _, _, row, lo, hi = name
            for s in range(lo, hi):
                chunk = 8 * row + s if row < 3 else PATH[ROWS[row]] if row < 7 and s == 0 else None
                if chunk is not None:
                    for r in (0, 1):
                        picked[half, r, row, s] = pick(half, chunk, 8 + r)
            span = pl.ds(lo, hi - lo)
            src = picked.at[half, 1, row, span]
            dst = sel_out.at[1, half, row, span]
            keep = pltpu.make_async_copy(
                picked.at[half, 0, row, span], sel_out.at[0, half, row, span], csem.at[len(locals_)]
            )
            keep.start()
            locals_.append(keep)
        elif kind == "G":
            sign = name[2]
            if sign > 0:
                for k in (0, 1):
                    extra[half, k] = full[half][glob[half, k] // 4, glob[half, k] % 4]
                keep = pltpu.make_async_copy(extra.at[half], cand_out.at[0, half, 0], csem.at[len(locals_)])
                keep.start()
                locals_.append(keep)
                j = 14 + half
                tail.append(
                    remote(extra.at[half], cand_out.at[1, half, 0], osend.at[j], orecv.at[j], peers["p"])
                )
                tail[-1].start()
            src = extra.at[half]
            dst = cand_out.at[0, half, 2 if sign > 0 else 1]
        else:
            sign = name[2]
            at = 2 if sign > 0 else 1
            src = cand_out.at[0, half, at]
            dst = cand_out.at[1, half, at]
        copy = remote(src, dst, send.at[i], recv.at[i], peer)
        copy.start()
        started[name] = copy
    wait_for(started)
    for copy in xcopies + ocopies + list(started.values()):
        copy.wait_send()
    for copy in tail + locals_:
        copy.wait()


def gather_all(keys, values, rand, want, glob):
    count = len(GATHER)
    keeps = 2 + sum(task[0][0] == "P" for task in GATHER)
    hbm = pl.BlockSpec(memory_space=pl.ANY)
    vmem = pl.BlockSpec(memory_space=pltpu.VMEM)
    smem = pl.BlockSpec(memory_space=pltpu.SMEM)
    return pl.pallas_call(
        gather_kernel,
        out_shape=(
            jax.ShapeDtypeStruct((2, 2, 8, 8, BLOCK, DH), BF16),
            jax.ShapeDtypeStruct((2, 6, BLOCK, DH), BF16),
            jax.ShapeDtypeStruct((2, 2, 3, 2, BLOCK, DH), BF16),
            jax.ShapeDtypeStruct(rand.shape, jnp.int32),
            jax.ShapeDtypeStruct((10,) + want.shape, jnp.int32),
        ),
        in_specs=[vmem] * 4 + [smem],
        out_specs=(hbm, hbm, hbm, vmem, vmem),
        scratch_shapes=[
            pltpu.VMEM((CHUNKS, 4, BLOCK, DH), BF16),
            pltpu.VMEM((CHUNKS, 4, BLOCK, DH), BF16),
            pltpu.VMEM((2, 2, 8, 8, BLOCK, DH), BF16),
            pltpu.VMEM((2, 2, 8, 8, BLOCK, DH), BF16),
            pltpu.VMEM((2, 2, BLOCK, DH), BF16),
            pltpu.SMEM((10,) + want.shape, jnp.int32),
            pltpu.SemaphoreType.DMA((count,)),
            pltpu.SemaphoreType.DMA((count,)),
            pltpu.SemaphoreType.DMA((3, 2)),
            pltpu.SemaphoreType.DMA((3, 2)),
            pltpu.SemaphoreType.DMA((16,)),
            pltpu.SemaphoreType.DMA((16,)),
            pltpu.SemaphoreType.DMA((3,)),
            pltpu.SemaphoreType.DMA((keeps,)),
        ],
        compiler_params=pltpu.CompilerParams(collective_id=1, has_side_effects=True),
        name="gather_blocks",
    )(keys, values, rand, want, glob)


def scatter_kernel(
    index, leaf_index, wants, glob, table, own, halo, dk, dv,
    mirror, staged, landed, line, origin, path, stem, gsum, gin, extra, rim, final,
    send, recv, xsend, xrecv, psem, hsem, lsem,
):
    seq, head, z, y, core = place()
    peers = neighbours(seq, head, z, y, core)
    enter(peers, seq, head)
    first = [remote(table, mirror, psem.at[0], psem.at[1], peers["p"])]
    for half in (0, 1):
        i = 2 * half
        first.append(remote(halo.at[half, 0], rim.at[half, 1], hsem.at[0, i], hsem.at[1, i], peers["last"]))
        first.append(
            remote(halo.at[half, 1], rim.at[half, 0], hsem.at[0, i + 1], hsem.at[1, i + 1], peers["next"])
        )
    for copy in first:
        copy.start()
    first[0].wait_recv()
    for half in (0, 1):
        for k in (0, 1):
            gsum[half, k] = (table[half, 32 + k].astype(F32) + mirror[half, 32 + k].astype(F32)).astype(BF16)

    started = {}
    waited = set()
    ready = set()

    def block_sum(half, chunk, sides, b):
        far, near = chunk_offsets(chunk)
        owner = owner_of(half, z, y, core, far, near)
        spot = (half * CHUNKS + chunk) * 4 + b
        total = table[half, index[0, spot]].astype(F32) + mirror[half, index[1, spot]].astype(F32)
        kind = sum(1 if sign > 0 else 2 for _, sign in sides)
        number = owner * 4 + b
        total += jnp.where(
            number == glob[0],
            extra[half, kind, 0],
            jnp.where(number == glob[1], extra[half, kind, 1], 0.0),
        )
        major = axis_of(half, True)
        for to, sign in sides:
            for r in (0, 1):
                inner = wants[SIDES[major, sign] * 2 + r, 0, owner]
                term = landed[half, r, to, chunk % 8].astype(F32)
                total += jnp.where(inner == b, term, 0.0)
        return total

    for name, link, _, deps in SCATTER:
        for dep in deps:
            if dep not in waited:
                waited.add(dep)
                started[dep].wait_recv()
        kind, half = name[:2]
        if kind in "mHF" and half not in ready:
            ready.add(half)
            for k in (0, 1):
                alone = table[half, 32 + k].astype(F32) + mirror[half, 32 + k].astype(F32)
                up, down = gin[half, 0, k].astype(F32), gin[half, 1, k].astype(F32)
                extra[half, 0, k] = alone
                extra[half, 1, k] = alone + up
                extra[half, 2, k] = alone + down
                extra[half, 3, k] = alone + up + down
        if kind == "F":
            for copy in first[1 + 2 * half : 3 + 2 * half]:
                copy.wait_recv()

            for b in range(4):
                total = block_sum(half, 0, [], b) + own[half, b]
                total += line[half, 0, 0, b].astype(F32) + origin[half, 0, b].astype(F32)
                total += stem[half, 0, b].astype(F32) + stem[half, 1, b].astype(F32)
                if b in (0, 3):
                    total += rim[half, b // 3].astype(F32)
                final[half, b] = total.astype(BF16)
            continue
        if kind == "G":
            src, dst = gsum.at[half], gin.at[half, 1 if name[2] > 0 else 0]
        elif kind == "L":
            _, _, to, sign, lo, hi = name
            for s in range(lo, hi):
                for r, terms in ((0, table), (1, mirror)):
                    staged[half, r, to, s] = terms[half, leaf_index[r, (half * 8 + to) * 8 + s]]
            span = pl.ds(lo, hi - lo)
            src, dst = staged.at[half, :, to, span], landed.at[half, :, to, span]
        elif kind == "m":
            _, _, row, sign, step = name
            slot = 7 if step == 4 else SLOT[sign * step]
            arrived = any(dep[0] == "m" for dep in deps)
            sides = children(row, slot)

            @pl.loop(0, 4)
            def _(b):
                total = block_sum(half, 8 * row + slot, sides, b)
                if arrived:
                    total += line[half, row, slot, b].astype(F32)
                line[half, row, slot, b] = total.astype(BF16)

            src = line.at[half, row, slot]
            if step > 1:
                dst = line.at[half, row, SLOT[sign * (step - 1)]]
            else:
                dst = line.at[half, row, 0] if sign > 0 else origin.at[half, row]
        else:
            _, _, sign, step = name
            if step == 3:
                row = 1 if sign > 0 else 2
                sides = children(row, 0)

                @pl.loop(0, 4)
                def _(b):
                    total = block_sum(half, 8 * row, sides, b)
                    total += line[half, row, 0, b].astype(F32) + origin[half, row, b].astype(F32)
                    line[half, row, 0, b] = total.astype(BF16)

                src = line.at[half, row, 0]
            else:
                chunk = PATH[sign * step]

                @pl.loop(0, 4)
                def _(b):
                    total = block_sum(half, chunk, [], b) + path[half, chunk - 24, b].astype(F32)
                    path[half, chunk - 24, b] = total.astype(BF16)

                src = path.at[half, chunk - 24]
            if step > 1:
                dst = path.at[half, PATH[sign * (step - 1)] - 24]
            else:
                dst = stem.at[half, 0 if sign > 0 else 1]
        i = SCATTER_SENDS[name]
        copy = remote(src, dst, send.at[i], recv.at[i], peers[link[0], link[1], 0])
        copy.start()
        started[name] = copy

    here = pl.ds(pl.multiple_of(head * DH, DH), DH)
    copies = []
    for j in (1, 2, 3):
        to = lax.rem(head + j, KVH)
        for n, target in enumerate((dk, dv)):
            copies.append(
                remote(
                    final.at[n, to],
                    target.at[:, here],
                    xsend.at[j - 1, n],
                    xrecv.at[j - 1, n],
                    {"seq": seq, "head": to},
                )
            )
            copies[-1].start()
    for n, target in enumerate((dk, dv)):
        copies.append(pltpu.make_async_copy(final.at[n, head], target.at[:, here], lsem.at[n]))
        copies[-1].start()
    for copy in copies:
        copy.wait()
    for copy in first + list(started.values()):
        copy.wait_send()


def scatter_all(index, leaf_index, wants, glob, table, own, halo):
    count = len(SCATTER_SENDS)
    vmem = pl.BlockSpec(memory_space=pltpu.VMEM)
    smem = pl.BlockSpec(memory_space=pltpu.SMEM)
    tile = (BLOCK, DH)
    return pl.pallas_call(
        scatter_kernel,
        out_shape=(jax.ShapeDtypeStruct((BLOCK, KVH * DH), BF16),) * 2,
        in_specs=[smem] * 4 + [vmem] * 3,
        out_specs=(pl.BlockSpec(memory_space=pl.ANY),) * 2,
        scratch_shapes=[
            pltpu.VMEM((2, TERMS) + tile, BF16),
            pltpu.VMEM((2, 2, 8, 8) + tile, BF16),
            pltpu.VMEM((2, 2, 8, 8) + tile, BF16),
            pltpu.VMEM((2, 3, 8, 4) + tile, BF16),
            pltpu.VMEM((2, 3, 4) + tile, BF16),
            pltpu.VMEM((2, 4, 4) + tile, BF16),
            pltpu.VMEM((2, 2, 4) + tile, BF16),
            pltpu.VMEM((2, 2) + tile, BF16),
            pltpu.VMEM((2, 2, 2) + tile, BF16),
            pltpu.VMEM((2, 4, 2) + tile, F32),
            pltpu.VMEM((2, 2) + tile, BF16),
            pltpu.VMEM((2, 4) + tile, BF16),
            pltpu.SemaphoreType.DMA((count,)),
            pltpu.SemaphoreType.DMA((count,)),
            pltpu.SemaphoreType.DMA((3, 2)),
            pltpu.SemaphoreType.DMA((3, 2)),
            pltpu.SemaphoreType.DMA((2,)),
            pltpu.SemaphoreType.DMA((2, 4)),
            pltpu.SemaphoreType.DMA((2,)),
        ],
        compiler_params=pltpu.CompilerParams(collective_id=2, has_side_effects=True),
        name="scatter_terms",
    )(index, leaf_index, wants, glob, table, own, halo)


def attention_kernel(
    spots, edges, same, queries, d_out, selected, nearby, candidates,
    out, dq, table, own, halo, kv, near, glob, sems, gsems,
):
    copies = [pltpu.make_async_copy(nearby.at[n], kv.at[n, pl.ds(0, 6)], gsems.at[n]) for n in (0, 1)]
    for n in (0, 1):
        for k in (0, 1):
            copies.append(
                pltpu.make_async_copy(candidates.at[spots[n, k]], kv.at[n, 6 + k], gsems.at[2 + 2 * n + k])
            )
    for copy in copies:
        copy.start()

    def fetch(e, n):
        return pltpu.make_async_copy(selected.at[spots[n, 2 + e]], kv.at[n, 8 + e], sems.at[n, e])

    for e in range(4 * RAND):
        for n in (0, 1):
            fetch(e, n).start()
    near[...] = jnp.zeros_like(near)
    glob[...] = jnp.zeros_like(glob)
    for n in (0, 1):
        table[n, NO_TERM:] = jnp.zeros((TERMS - NO_TERM, BLOCK, DH), BF16)
    for copy in copies:
        copy.wait()
    for e in range(4 * RAND):
        for n in (0, 1):
            fetch(e, n).wait()
    factor = DH ** (-0.5)
    dims = lambda a, b: (((a,), (b,)), ((), ()))

    def dot(a, b, at, bt):
        return lax.dot_general(a, b, dims(at, bt), preferred_element_type=F32)

    @pl.loop(0, 4)
    def _(i):
        rows = pl.ds(pl.multiple_of(i * BLOCK, BLOCK), BLOCK)
        stack = lambda ref: jnp.concatenate(
            [ref[rows, h * DH : (h + 1) * DH] for h in range(HEADS)], axis=0
        )
        q, g = stack(queries), stack(d_out)

        def listed(n):
            return jnp.concatenate(
                [
                    kv[n, pl.ds(i, 3)].reshape(3 * BLOCK, DH),
                    kv[n, 6:8].reshape(2 * BLOCK, DH),
                    kv[n, pl.ds(8 + i * RAND, RAND)].reshape(RAND * BLOCK, DH),
                ],
                axis=0,
            )

        k, v = listed(0), listed(1)
        scores = dot(k, q, 1, 1) * factor
        cut_first = jnp.logical_and(i == 0, edges[0] == 1)
        cut_last = jnp.logical_and(i == 3, edges[1] == 1)
        scores = jnp.concatenate(
            [
                jnp.where(cut_first, NEG_FILL, scores[:BLOCK]),
                scores[BLOCK : 2 * BLOCK],
                jnp.where(cut_last, NEG_FILL, scores[2 * BLOCK : 3 * BLOCK]),
                scores[3 * BLOCK :],
            ],
            axis=0,
        )
        peak = jnp.max(scores, axis=0, keepdims=True)
        weights = jnp.exp(scores - peak)
        probs = weights * (1.0 / jnp.sum(weights, axis=0, keepdims=True))
        probs16 = probs.astype(BF16)
        result = dot(v, probs16, 0, 0).astype(BF16)
        delta = jnp.sum(g.T.astype(F32) * result.astype(F32), axis=0, keepdims=True)
        dprobs = dot(v, g, 1, 1)
        dscores = (probs * (dprobs - delta)).astype(BF16)
        dquery = (dot(k, dscores, 0, 0) * factor).astype(BF16).T
        result = result.T
        for h in range(HEADS):
            out[rows, h * DH : (h + 1) * DH] = result[h * BLOCK : (h + 1) * BLOCK]
            dq[rows, h * DH : (h + 1) * DH] = dquery[h * BLOCK : (h + 1) * BLOCK]
        for n, terms in ((0, dot(dscores, q, 1, 0) * factor), (1, dot(probs16, g, 1, 0))):
            near[n, pl.ds(i, 3)] += terms[: 3 * BLOCK].reshape(3, BLOCK, DH)
            glob[n] += terms[3 * BLOCK : 5 * BLOCK].reshape(2, BLOCK, DH)
            table[n, pl.ds(i * RAND, RAND)] = terms[5 * BLOCK :].astype(BF16).reshape(RAND, BLOCK, DH)

    for n in (0, 1):
        own[n] = near[n, 1:5]
        halo[n, 0] = near[n, 0].astype(BF16)
        halo[n, 1] = near[n, 5].astype(BF16)
        for a in (0, 1):
            total = glob[n, a] + jnp.where(same[0] == 1, glob[n, 1 - a], 0.0)
            table[n, 32 + a] = total.astype(BF16)


def attention(spots, edges, same, queries, d_out, selected, nearby, candidates):
    smem = pl.BlockSpec(memory_space=pltpu.SMEM)
    vmem = pl.BlockSpec(memory_space=pltpu.VMEM)
    tile = (BLOCK, DH)
    return pl.pallas_call(
        attention_kernel,
        out_shape=(
            jax.ShapeDtypeStruct(queries.shape, BF16),
            jax.ShapeDtypeStruct(queries.shape, BF16),
            jax.ShapeDtypeStruct((2, TERMS) + tile, BF16),
            jax.ShapeDtypeStruct((2, 4) + tile, F32),
            jax.ShapeDtypeStruct((2, 2) + tile, BF16),
        ),
        in_specs=[smem] * 3 + [vmem] * 2 + [pl.BlockSpec(memory_space=pl.ANY)] * 3,
        out_specs=(vmem,) * 5,
        scratch_shapes=[
            pltpu.VMEM((2, KV_ROWS) + tile, BF16),
            pltpu.VMEM((2, 6) + tile, F32),
            pltpu.VMEM((2, 2) + tile, F32),
            pltpu.SemaphoreType.DMA((2, 4 * RAND)),
            pltpu.SemaphoreType.DMA((6,)),
        ],
        compiler_params=pltpu.CompilerParams(vmem_limit_bytes=60 * 1024 * 1024),
        name="block_attention",
    )(spots, edges, same, queries, d_out, selected, nearby, candidates)


def chosen(value, table):
    result = jnp.full_like(value, table[0])
    for i, entry in enumerate(table[1:], 1):
        result = jnp.where(value == i, entry, result)
    return result


SLOTS_MOD = [SLOT[d] if d <= 4 else SLOT[d - RING] for d in range(RING)]
ROWS_MOD = [ROWS.index(d) if d <= 4 else ROWS.index(d - RING) for d in range(RING)]


def relation(z, y, owner, half):
    dz = (z - owner // 16) % RING
    dy = (y - (owner // 2) % RING) % RING
    far = jnp.where(half == 0, dz, dy)
    near = jnp.where(half == 0, dy, dz)
    return chosen(far, ROWS_MOD), chosen(near, SLOTS_MOD)


def body(queries, keys, values, d_out, rand_blocks, glob_blocks):
    seq, head, z, y, core = place()
    seq_count = lax.axis_size("seq")
    ints = lambda n: jnp.arange(n, dtype=jnp.int32)
    rand = rand_blocks.reshape(-1)
    owners = ints(seq_count)
    hits = jnp.where(rand[:, None] // 4 == owners[None, :], rand[:, None] % 4, 0)
    want = jnp.max(hits, axis=0)[None, :]

    halves = ints(2)[:, None]
    grow, gslot = relation(z, y, glob_blocks[None, :] // 4, halves)
    whole = jnp.where(grow < 3, grow * 8 + gslot, 24 + grow - 3)
    is_whole = (grow < 3) | ((gslot == 0) & (grow < 7))
    glob_at = jnp.where(is_whole, whole * 4 + glob_blocks[None, :] % 4, 0)
    selected, nearby, candidates, partner_rand, wants = gather_all(keys, values, rand_blocks, want, glob_at)

    away = (glob_blocks // 4 % 2 != core).astype(jnp.int32)[None, :]
    late = (gslot >= 3) & (gslot < 7)
    parent = chosen(grow, [0, 0, 0, 2, 1, 1, 2, 2])
    parent = jnp.where((grow == 7) & late, 1, parent)
    parent = jnp.where(is_whole, 0, parent)
    glob_spots = ((away * 2 + halves) * 3 + parent) * 2 + ints(2)[None, :]
    row, slot = relation(z, y, rand[None, :] // 4, halves)
    away = (rand // 4 % 2 != core).astype(jnp.int32)[None, :]
    rand_spots = ((away * 2 + halves) * 8 + row) * 8 + slot
    spots = jnp.concatenate([glob_spots, rand_spots], axis=1)
    edges = jnp.stack([seq == 0, seq == seq_count - 1]).astype(jnp.int32)
    same = (glob_blocks[:1] == glob_blocks[1:]).astype(jnp.int32)
    out, dq, table, own, halo = attention(
        spots,
        edges,
        same,
        queries,
        d_out,
        selected.reshape(256, BLOCK, DH),
        nearby,
        candidates.reshape(24, BLOCK, DH),
    )

    def owner_at(half, far, near):
        oz = (z - jnp.where(half == 0, far, near)) % RING
        oy = (y - jnp.where(half == 0, near, far)) % RING
        return oz * 16 + oy * 2 + core

    def lookup(ids, targets):
        numbers = ints(32)
        match = jnp.where(targets[None, :] == ids[:, None], numbers[:, None], NO_TERM)
        return jnp.min(match, axis=0)

    flat = ints(2 * CHUNKS * 4)
    half, chunk = flat // (CHUNKS * 4), flat // 4 % CHUNKS
    far = jnp.where(chunk < 24, chosen(chunk // 8, ROWS[:3]), chosen(chunk - 24, (1, -1, 2, -2)))
    near = jnp.where(chunk < 24, chosen(chunk % 8, ORDER), 0)
    block = owner_at(half, far, near) * 4 + flat % 4
    theirs = partner_rand.reshape(-1)
    index = jnp.stack([lookup(rand, block), lookup(theirs, block)])
    flat = ints(128)
    owner = owner_at(flat // 64, chosen(flat // 8 % 8, ROWS), chosen(flat % 8, ORDER))
    leaf_index = jnp.stack([lookup(rand // 4, owner), lookup(theirs // 4, owner)])
    dk, dv = scatter_all(index, leaf_index, wants, glob_blocks, table, own, halo)
    return (out, dq, dk, dv)


def solution(mesh):
    in_specs = (
        P("seq", "head"),
        P(("seq", "head"), None),
        P(("seq", "head"), None),
        P("seq", "head"),
        P("seq", None),
        P(),
    )
    out_specs = (
        P("seq", "head"),
        P("seq", "head"),
        P(("seq", "head"), None),
        P(("seq", "head"), None),
    )
    return jax.shard_map(body, mesh=mesh, in_specs=in_specs, out_specs=out_specs, check_vma=False)
```

```python
import jax
import jax.numpy as jnp
from jax import lax
from jax.experimental import pallas as pl
from jax.experimental.pallas import tpu as pltpu
from jax.sharding import PartitionSpec as P

DH = 128
KVH = 4
HEADS = 8
BLOCK = 64
RAND = 8
PAIR = 2 * DH
RING = 8
NEG_FILL = -1e30
BF16 = jnp.bfloat16
F32 = jnp.float32
MESH = pl.DeviceIdType.MESH

ORDER = (0, 1, -1, 2, -2, 3, -3, 4)
SLOT = {d: i for i, d in enumerate(ORDER)}
ROWS = (0, 3, -3, 1, -1, 2, -2, 4)
PATH = {1: 24, -1: 25, 2: 26, -2: 27}
CHUNKS = 28
INNER = ((1, 3), (3, 5), (5, 7), (7, 8))
LEAVES = (
    (1, 1, 7, ((0, 3), (7, 8))),
    (2, -1, 7, ((3, 5), (5, 7))),
    (1, -1, 5, INNER),
    (2, 1, 6, INNER),
    (0, 1, 3, INNER),
    (0, -1, 4, INNER),
)
SIDES = {("z", 1): 0, ("z", -1): 1, ("y", 1): 2, ("y", -1): 3}
CHUNK_US = 1.78
HALF_US = 0.05
HOP_US = 2.8
TABLE_US = 3.0
KV_ROWS = 40
TERMS = 36
NO_TERM = 34
WANT = (1, 2 * RING * RING)


def axis_of(half, major):
    return "zy"[half] if major else "yz"[half]


def ordered(tasks):
    followers = {}
    for task in tasks:
        for dep in task[3]:
            followers.setdefault(dep, []).append(task)
    left = {}

    def remaining(task):
        if task[0] not in left:
            after = max((remaining(t) for t in followers.get(task[0], ())), default=0.0)
            left[task[0]] = task[2] + HOP_US + after
        return left[task[0]]

    arrival, free, result = {}, {}, []
    waiting = list(tasks)
    while waiting:
        best = None
        for task in waiting:
            if all(dep in arrival for dep in task[3]):
                ready = max([arrival[dep] for dep in task[3]], default=0.0)
                key = (max(ready, free.get(task[1], 0.0)), -remaining(task))
                if best is None or key < best[0]:
                    best = (key, task)
        (start, _), task = best
        waiting.remove(task)
        name, link, time, deps = task
        free[link] = start + time
        arrival[name] = start + time + HOP_US
        result.append(task)
    return result, max(arrival.values())


def far_sign(half, row):
    return 1 if (half + row) % 2 == 0 else -1


def gather_tasks():
    tasks = []
    for half in (0, 1):
        minor, major = axis_of(half, False), axis_of(half, True)
        whole, leaf = {}, {}
        for step in range(3):
            for sign in (1, -1):
                name = ("H", half, sign, step)
                deps = (("H", half, sign, step - 1),) if step else ()
                tasks.append((name, (major, sign), CHUNK_US, deps))
                if step < 2:
                    whole[PATH[sign * (step + 1)]] = name
                else:
                    whole[8 if sign > 0 else 16] = name
        for row in range(3):
            far = far_sign(half, row)
            for sign in (1, -1):
                for step in range(4 if sign == far else 3):
                    name = ("m", half, row, sign, step)
                    if step:
                        deps = (("m", half, row, sign, step - 1),)
                    else:
                        deps = (whole[8 * row],) if row else ()
                    tasks.append((name, (minor, sign), CHUNK_US, deps))
                    to = 7 if step == 3 else SLOT[sign * (step + 1)]
                    whole[8 * row + to] = name
        for row, sign, to, ranges in LEAVES:
            for lo, hi in ranges:
                name = ("L", half, row, sign, to, lo, hi)
                deps = tuple(whole[8 * row + s] for s in range(lo, hi) if row or s)
                tasks.append((name, (major, sign), CHUNK_US * (hi - lo) / 2, deps))
                for s in range(lo, hi):
                    leaf[to, s] = name
        copies = tuple(whole.values())
        for sign in (1, -1):
            tasks.append((("G", half, sign), (major, sign), CHUNK_US / 2, copies))
        for sign in (1, -1):
            tasks.append((("X", half, sign), "p", HALF_US, (("G", half, sign),)))
        for row in range(8):
            groups = ((0, 5), (5, 8)) if row < 7 else ((0, 3), (3, 7), (7, 8))
            for lo, hi in groups:
                deps = []
                for s in range(lo, hi):
                    if row < 3:
                        deps.append(whole.get(8 * row + s))
                    elif row < 7 and s == 0:
                        deps.append(whole[PATH[ROWS[row]]])
                    else:
                        deps.append(leaf[row, s])
                deps = tuple(dict.fromkeys(d for d in deps if d))
                tasks.append((("P", half, row, lo, hi), "p", HALF_US * (hi - lo), deps))
    late = [task for task in ordered(tasks)[0] if task[0][0] in "PX"]
    result, seen = [], set()
    for task in ordered([task for task in tasks if task[0][0] not in "PX"])[0]:
        result.append(task)
        seen.update(task[3])
        for other in [t for t in late if set(t[3]) <= seen]:
            late.remove(other)
            result.append(other)
    return result + late


def children(row, slot):
    if row == 0:
        return [(3, 1), (4, -1)] if slot else []
    result = []
    if slot:
        result.append((5, -1) if row == 1 else (6, 1))
    if row == 1 and slot in (0, 1, 2, 7):
        result.append((7, 1))
    if row == 2 and slot in (3, 4, 5, 6):
        result.append((7, -1))
    return result


def scatter_tasks():
    tasks = [(("T", 0), "p", TABLE_US, ())]
    for half in (0, 1):
        major = axis_of(half, True)
        for sign in (1, -1):
            tasks.append((("G", half, sign), (major, sign), CHUNK_US / 2, (("T", 0),)))
    leaf = {}
    for row, sign, to, ranges in LEAVES:
        for lo, hi in reversed(ranges):
            for half in (0, 1):
                major = axis_of(half, True)
                for r in (0, 1):
                    name = ("L", half, to, sign, lo, hi, r)
                    deps = (("T", 0),) if r else ()
                    tasks.append((name, (major, -sign), CHUNK_US * (hi - lo) / 4, deps))
                    for s in range(lo, hi):
                        leaf[half, to, s, r] = name
    for half in (0, 1):
        minor, major = axis_of(half, False), axis_of(half, True)
        extra = (("G", half, 1), ("G", half, -1))

        def leaves(row, slot):
            return tuple(leaf[half, to, slot, r] for to, _ in children(row, slot) for r in (0, 1)) + extra

        for row in (1, 2, 0):
            for sign in (1, -1):
                top = 4 if sign == far_sign(half, row) else 3
                for step in range(top, 0, -1):
                    deps = leaves(row, 7 if step == 4 else SLOT[sign * step])
                    if step < top:
                        deps += (("m", half, row, sign, step + 1),)
                    tasks.append((("m", half, row, sign, step), (minor, -sign), CHUNK_US, deps))
        for sign in (1, -1):
            row = 1 if sign > 0 else 2
            for step in (3, 2, 1):
                if step == 3:
                    deps = leaves(row, 0) + (("m", half, row, 1, 1), ("m", half, row, -1, 1))
                else:
                    deps = (("H", half, sign, step + 1),)
                tasks.append((("H", half, sign, step), (major, -sign), CHUNK_US, deps))
        deps = tuple((k, half, s, 1) for k in "H" for s in (1, -1))
        deps += (("m", half, 0, 1, 1), ("m", half, 0, -1, 1))
        tasks.append((("F", half), ("f", half), 0.0, deps))
    return ordered(tasks)[0]


GATHER = gather_tasks()
SCATTER = scatter_tasks()
GATHER_SENDS = {task[0]: i for i, task in enumerate(GATHER)}
SCATTER_SENDS = {t[0]: i for i, t in enumerate(t for t in SCATTER if t[0][0] != "F")}


def place():
    seq = lax.axis_index("seq")
    head = lax.axis_index("head")
    return seq, head, seq // 16, (seq // 2) % RING, seq % 2


def neighbours(seq, head, z, y, core):
    up = lambda v: lax.rem(v + 1, RING)
    down = lambda v: lax.rem(v + RING - 1, RING)
    index = lambda zz, yy, cc: zz * 16 + yy * 2 + cc
    count = 2 * RING * RING
    peers = {}
    for name, cc in ((0, core), (1, 1 - core)):
        peers["z", 1, name] = index(up(z), y, cc)
        peers["z", -1, name] = index(down(z), y, cc)
        peers["y", 1, name] = index(z, up(y), cc)
        peers["y", -1, name] = index(z, down(y), cc)
    peers["p"] = index(z, y, 1 - core)
    peers["next"] = lax.rem(seq + 1, count)
    peers["last"] = lax.rem(seq + count - 1, count)
    return {k: {"seq": v, "head": head} for k, v in peers.items()}


def enter(peers, seq, head):
    barrier = pltpu.get_barrier_semaphore()
    everyone = list(peers.values())
    everyone += [{"seq": seq, "head": lax.rem(head + j, KVH)} for j in (1, 2, 3)]
    for peer in everyone:
        pl.semaphore_signal(barrier, inc=1, device_id=peer, device_id_type=MESH)
    pl.semaphore_wait(barrier, len(everyone))


def remote(src, dst, send, recv, peer):
    return pltpu.make_async_remote_copy(
        src_ref=src,
        dst_ref=dst,
        send_sem=send,
        recv_sem=recv,
        device_id=peer,
        device_id_type=MESH,
    )


def owner_of(half, z, y, core, far, near):
    dz, dy = (far, near) if half == 0 else (near, far)
    return lax.rem(z - dz + RING, RING) * 16 + lax.rem(y - dy + RING, RING) * 2 + core


def chunk_offsets(chunk):
    if chunk < 24:
        return ROWS[chunk // 8], ORDER[chunk % 8]
    return (1, -1, 2, -2)[chunk - 24], 0


def chosen(value, table):
    result = table[0]
    for i, entry in enumerate(table[1:], 1):
        result = jnp.where(value == i, entry, result)
    return result


SLOTS_MOD = [SLOT[d] if d <= 4 else SLOT[d - RING] for d in range(RING)]
ROWS_MOD = [ROWS.index(d) if d <= 4 else ROWS.index(d - RING) for d in range(RING)]
PARENT = [0, 0, 0, 2, 1, 1, 2, 2]


def relation(z, y, owner, half):
    dz = (z + RING - owner // 16) % RING
    dy = (y + RING - (owner // 2) % RING) % RING
    far, near = (dz, dy) if half == 0 else (dy, dz)
    return chosen(far, ROWS_MOD), chosen(near, SLOTS_MOD)


def gather_kernel(
    keys, values, rand, glob, sel_out, near_out, cand_out, wants, want,
    full0, full1, picked, staged, extra, scal, send, recv, xsend, xrecv, osend, orecv, lsem, csem,
):
    seq, head, z, y, core = place()
    peers = neighbours(seq, head, z, y, core)
    full = (full0, full1)
    lane = lax.broadcasted_iota(jnp.int32, (1, 2 * RING * RING), 1)
    named = jnp.full_like(lane, 4 * NO_TERM)
    for e in range(4 * RAND):
        block = rand[e // RAND, e % RAND]
        named = jnp.where(lane == block // 4, 4 * e + block % 4, named)
    want[...] = named
    local = pltpu.make_async_copy(want, wants.at[8], lsem.at[0])
    local.start()
    local.wait()
    enter(peers, seq, head)
    pieces = (keys, values)
    xcopies = []
    for j in (1, 2, 3):
        to = lax.rem(head + j, KVH)
        for n, source in enumerate(pieces):
            xcopies.append(
                remote(
                    source.at[:, pl.ds(pl.multiple_of(to * DH, DH), DH)],
                    full[n].at[0, head],
                    xsend.at[j - 1, n],
                    xrecv.at[j - 1, n],
                    {"seq": seq, "head": to},
                )
            )
            xcopies[-1].start()
    ocopies = [remote(wants.at[8], wants.at[9], osend.at[0], orecv.at[0], peers["p"])]
    for (axis, sign), side in SIDES.items():
        back = SIDES[axis, -sign] * 2
        for r in (0, 1):
            i = len(ocopies)
            peer = peers[axis, sign, r]
            ocopies.append(remote(wants.at[8], wants.at[back + r], osend.at[i], orecv.at[i], peer))
    for copy in ocopies:
        copy.start()
    local = []
    for n, source in enumerate(pieces):
        mine = source.at[:, pl.ds(pl.multiple_of(head * DH, DH), DH)]
        local.append(pltpu.make_async_copy(mine, full[n].at[0, head], lsem.at[1 + n]))
    for copy in local:
        copy.start()
    for copy in local:
        copy.wait()
    for copy in xcopies:
        copy.wait_recv()

    started = {}
    waited = set()
    tail = []

    def wait_for(deps):
        for dep in deps:
            if dep not in waited:
                waited.add(dep)
                started[dep].wait_recv()

    def finish_start():
        for copy in ocopies:
            copy.wait_recv()
        scalars = pltpu.make_async_copy(wants, scal, lsem.at[0])
        scalars.start()
        for half in (0, 1):
            i = 10 + 2 * half
            tail.append(remote(full[half].at[0, 3], near_out.at[half, 0], osend.at[i], orecv.at[i], peers["next"]))
            tail.append(
                remote(full[half].at[0, 0], near_out.at[half, 5], osend.at[i + 1], orecv.at[i + 1], peers["last"])
            )
            tail.append(
                pltpu.make_async_copy(full[half].at[0], near_out.at[half, pl.ds(1, 4)], lsem.at[1 + half])
            )
        for copy in tail:
            copy.start()
        scalars.wait()

    def pick(half, chunk, side):
        far, near = chunk_offsets(chunk)
        inner = scal[side, 0, owner_of(half, z, y, core, far, near)] % 4
        block = full[half][chunk, 0]
        for b in (1, 2, 3):
            block = jnp.where(inner == b, full[half][chunk, b], block)
        return block

    ready = False
    passed = set()
    locals_ = []
    for name, link, _, deps in GATHER:
        wait_for(deps)
        kind, half = name[:2]
        major = axis_of(half, True)
        if kind in "LP" and not ready:
            finish_start()
            ready = True
        i = GATHER_SENDS[name]
        peer = peers["p"] if link == "p" else peers[link[0], link[1], 0]
        extra_sends = []
        if kind == "H":
            _, _, sign, step = name
            src = full[half].at[PATH[sign * step] if step else 0]
            dst = full[half].at[PATH[sign * (step + 1)] if step < 2 else (8 if sign > 0 else 16)]
        elif kind == "m":
            _, _, row, sign, step = name
            src = full[half].at[8 * row + SLOT[sign * step]]
            dst = full[half].at[8 * row + (7 if step == 3 else SLOT[sign * (step + 1)])]
        elif kind == "L":
            _, _, row, sign, to, lo, hi = name
            side = SIDES[major, sign] * 2
            for s in range(lo, hi):
                for r in (0, 1):
                    staged[half, r, to, s] = pick(half, 8 * row + s, side + r)
            src = staged.at[half, :, to, pl.ds(lo, hi - lo)]
            dst = picked.at[half, :, to, pl.ds(lo, hi - lo)]
        elif kind == "P":
            _, _, row, lo, hi = name
            for s in range(lo, hi):
                chunk = 8 * row + s if row < 3 else PATH[ROWS[row]] if row < 7 and s == 0 else None
                if chunk is not None:
                    for r in (0, 1):
                        picked[half, r, row, s] = pick(half, chunk, 8 + r)
            span = pl.ds(lo, hi - lo)
            src = picked.at[half, 1, row, span]
            dst = sel_out.at[1, half, row, span]
            keep = pltpu.make_async_copy(
                picked.at[half, 0, row, span], sel_out.at[0, half, row, span], csem.at[len(locals_)]
            )
            keep.start()
            locals_.append(keep)
        elif kind == "G":
            sign = name[2]
            if half not in passed:
                passed.add(half)
                for k in (0, 1):
                    row, slot = relation(z, y, glob[k] // 4, half)
                    chunk = jnp.where(row < 3, row * 8 + slot, jnp.where(row < 7, 21 + row, 0))
                    extra[half, k] = full[half][chunk, glob[k] % 4]
                keep = pltpu.make_async_copy(extra.at[half], cand_out.at[0, half, 0], csem.at[len(locals_)])
                keep.start()
                locals_.append(keep)
                j = 14 + half
                tail.append(
                    remote(extra.at[half], cand_out.at[1, half, 0], osend.at[j], orecv.at[j], peers["p"])
                )
                tail[-1].start()
            src = extra.at[half]
            dst = cand_out.at[0, half, 2 if sign > 0 else 1]
        else:
            sign = name[2]
            at = 2 if sign > 0 else 1
            src = cand_out.at[0, half, at]
            dst = cand_out.at[1, half, at]
        copy = remote(src, dst, send.at[i], recv.at[i], peer)
        copy.start()
        started[name] = copy
    wait_for(started)
    for copy in xcopies + ocopies + list(started.values()):
        copy.wait_send()
    for copy in tail + locals_:
        copy.wait()


def gather_all(keys, values, rand, glob):
    count = len(GATHER)
    keeps = 2 + sum(task[0][0] == "P" for task in GATHER)
    hbm = pl.BlockSpec(memory_space=pl.ANY)
    vmem = pl.BlockSpec(memory_space=pltpu.VMEM)
    smem = pl.BlockSpec(memory_space=pltpu.SMEM)
    return pl.pallas_call(
        gather_kernel,
        out_shape=(
            jax.ShapeDtypeStruct((2, 2, 8, 8, BLOCK, DH), BF16),
            jax.ShapeDtypeStruct((2, 6, BLOCK, DH), BF16),
            jax.ShapeDtypeStruct((2, 2, 3, 2, BLOCK, DH), BF16),
            jax.ShapeDtypeStruct((10,) + WANT, jnp.int32),
        ),
        in_specs=[vmem] * 2 + [smem] * 2,
        out_specs=(hbm, hbm, hbm, vmem),
        scratch_shapes=[
            pltpu.VMEM(WANT, jnp.int32),
            pltpu.VMEM((CHUNKS, 4, BLOCK, DH), BF16),
            pltpu.VMEM((CHUNKS, 4, BLOCK, DH), BF16),
            pltpu.VMEM((2, 2, 8, 8, BLOCK, DH), BF16),
            pltpu.VMEM((2, 2, 8, 8, BLOCK, DH), BF16),
            pltpu.VMEM((2, 2, BLOCK, DH), BF16),
            pltpu.SMEM((10,) + WANT, jnp.int32),
            pltpu.SemaphoreType.DMA((count,)),
            pltpu.SemaphoreType.DMA((count,)),
            pltpu.SemaphoreType.DMA((3, 2)),
            pltpu.SemaphoreType.DMA((3, 2)),
            pltpu.SemaphoreType.DMA((16,)),
            pltpu.SemaphoreType.DMA((16,)),
            pltpu.SemaphoreType.DMA((3,)),
            pltpu.SemaphoreType.DMA((keeps,)),
        ],
        compiler_params=pltpu.CompilerParams(collective_id=1, has_side_effects=True),
        name="gather_blocks",
    )(keys, values, rand, glob)


def scatter_kernel(
    wants, glob, table, own, halo, dk, dv,
    mirror, staged, landed, line, origin, path, stem, gsum, gin, extra, rim, final,
    send, recv, xsend, xrecv, hsem, lsem,
):
    seq, head, z, y, core = place()
    peers = neighbours(seq, head, z, y, core)
    enter(peers, seq, head)
    first = []
    for half in (0, 1):
        i = 2 * half
        first.append(remote(halo.at[half, 0], rim.at[half, 1], hsem.at[0, i], hsem.at[1, i], peers["last"]))
        first.append(
            remote(halo.at[half, 1], rim.at[half, 0], hsem.at[0, i + 1], hsem.at[1, i + 1], peers["next"])
        )
    started = {}
    waited = set()
    ready = set()
    passed = set()

    def block_sum(half, chunk, sides, b):
        far, near = chunk_offsets(chunk)
        owner = owner_of(half, z, y, core, far, near)
        mine, theirs = wants[8, 0, owner], wants[9, 0, owner]
        total = jnp.where(mine % 4 == b, table[half, mine // 4].astype(F32), 0.0)
        total += jnp.where(theirs % 4 == b, mirror[half, theirs // 4].astype(F32), 0.0)
        kind = sum(1 if sign > 0 else 2 for _, sign in sides)
        number = owner * 4 + b
        total += jnp.where(
            number == glob[0],
            extra[half, kind, 0],
            jnp.where(number == glob[1], extra[half, kind, 1], 0.0),
        )
        major = axis_of(half, True)
        for to, sign in sides:
            for r in (0, 1):
                inner = wants[SIDES[major, sign] * 2 + r, 0, owner] % 4
                term = landed[half, r, to, chunk % 8].astype(F32)
                total += jnp.where(inner == b, term, 0.0)
        return total

    for name, link, _, deps in SCATTER:
        for dep in deps:
            if dep not in waited:
                waited.add(dep)
                started[dep].wait_recv()
        kind, half = name[:2]
        if kind in "mHF" and half not in ready:
            ready.add(half)
            for k in (0, 1):
                alone = table[half, 32 + k].astype(F32) + mirror[half, 32 + k].astype(F32)
                up, down = gin[half, 0, k].astype(F32), gin[half, 1, k].astype(F32)
                extra[half, 0, k] = alone
                extra[half, 1, k] = alone + up
                extra[half, 2, k] = alone + down
                extra[half, 3, k] = alone + up + down
        if kind == "F":
            for copy in first[2 * half : 2 * half + 2]:
                copy.wait_recv()

            for b in range(4):
                total = block_sum(half, 0, [], b) + own[half, b]
                total += line[half, 0, 0, b].astype(F32) + origin[half, 0, b].astype(F32)
                total += stem[half, 0, b].astype(F32) + stem[half, 1, b].astype(F32)
                if b in (0, 3):
                    total += rim[half, b // 3].astype(F32)
                final[half, b] = total.astype(BF16)
            continue
        if kind == "T":
            src, dst = table, mirror
        elif kind == "G":
            if half not in passed:
                passed.add(half)
                for k in (0, 1):
                    alone = table[half, 32 + k].astype(F32) + mirror[half, 32 + k].astype(F32)
                    gsum[half, k] = alone.astype(BF16)
            src, dst = gsum.at[half], gin.at[half, 1 if name[2] > 0 else 0]
        elif kind == "L":
            _, _, to, sign, lo, hi, r = name
            for s in range(lo, hi):
                owner = owner_of(half, z, y, core, ROWS[to], ORDER[s])
                staged[half, r, to, s] = (table, mirror)[r][half, wants[8 + r, 0, owner] // 4]
            span = pl.ds(lo, hi - lo)
            src, dst = staged.at[half, r, to, span], landed.at[half, r, to, span]
        elif kind == "m":
            _, _, row, sign, step = name
            slot = 7 if step == 4 else SLOT[sign * step]
            arrived = any(dep[0] == "m" for dep in deps)
            sides = children(row, slot)

            @pl.loop(0, 4)
            def _(b):
                total = block_sum(half, 8 * row + slot, sides, b)
                if arrived:
                    total += line[half, row, slot, b].astype(F32)
                line[half, row, slot, b] = total.astype(BF16)

            src = line.at[half, row, slot]
            if step > 1:
                dst = line.at[half, row, SLOT[sign * (step - 1)]]
            else:
                dst = line.at[half, row, 0] if sign > 0 else origin.at[half, row]
        else:
            _, _, sign, step = name
            if step == 3:
                row = 1 if sign > 0 else 2
                sides = children(row, 0)

                @pl.loop(0, 4)
                def _(b):
                    total = block_sum(half, 8 * row, sides, b)
                    total += line[half, row, 0, b].astype(F32) + origin[half, row, b].astype(F32)
                    line[half, row, 0, b] = total.astype(BF16)

                src = line.at[half, row, 0]
            else:
                chunk = PATH[sign * step]

                @pl.loop(0, 4)
                def _(b):
                    total = block_sum(half, chunk, [], b) + path[half, chunk - 24, b].astype(F32)
                    path[half, chunk - 24, b] = total.astype(BF16)

                src = path.at[half, chunk - 24]
            if step > 1:
                dst = path.at[half, PATH[sign * (step - 1)] - 24]
            else:
                dst = stem.at[half, 0 if sign > 0 else 1]
        i = SCATTER_SENDS[name]
        peer = peers["p"] if link == "p" else peers[link[0], link[1], 0]
        copy = remote(src, dst, send.at[i], recv.at[i], peer)
        copy.start()
        started[name] = copy
        if kind == "T":
            for copy in first:
                copy.start()

    here = pl.ds(pl.multiple_of(head * DH, DH), DH)
    copies = []
    for j in (1, 2, 3):
        to = lax.rem(head + j, KVH)
        for n, target in enumerate((dk, dv)):
            copies.append(
                remote(
                    final.at[n, to],
                    target.at[:, here],
                    xsend.at[j - 1, n],
                    xrecv.at[j - 1, n],
                    {"seq": seq, "head": to},
                )
            )
            copies[-1].start()
    for n, target in enumerate((dk, dv)):
        copies.append(pltpu.make_async_copy(final.at[n, head], target.at[:, here], lsem.at[n]))
        copies[-1].start()
    for copy in copies:
        copy.wait()
    for copy in first + list(started.values()):
        copy.wait_send()


def scatter_all(wants, glob, table, own, halo):
    count = len(SCATTER_SENDS)
    vmem = pl.BlockSpec(memory_space=pltpu.VMEM)
    smem = pl.BlockSpec(memory_space=pltpu.SMEM)
    tile = (BLOCK, DH)
    return pl.pallas_call(
        scatter_kernel,
        out_shape=(jax.ShapeDtypeStruct((BLOCK, KVH * DH), BF16),) * 2,
        in_specs=[smem] * 2 + [vmem] * 3,
        out_specs=(pl.BlockSpec(memory_space=pl.ANY),) * 2,
        scratch_shapes=[
            pltpu.VMEM((2, TERMS) + tile, BF16),
            pltpu.VMEM((2, 2, 8, 8) + tile, BF16),
            pltpu.VMEM((2, 2, 8, 8) + tile, BF16),
            pltpu.VMEM((2, 3, 8, 4) + tile, BF16),
            pltpu.VMEM((2, 3, 4) + tile, BF16),
            pltpu.VMEM((2, 4, 4) + tile, BF16),
            pltpu.VMEM((2, 2, 4) + tile, BF16),
            pltpu.VMEM((2, 2) + tile, BF16),
            pltpu.VMEM((2, 2, 2) + tile, BF16),
            pltpu.VMEM((2, 4, 2) + tile, F32),
            pltpu.VMEM((2, 2) + tile, BF16),
            pltpu.VMEM((2, 4) + tile, BF16),
            pltpu.SemaphoreType.DMA((count,)),
            pltpu.SemaphoreType.DMA((count,)),
            pltpu.SemaphoreType.DMA((3, 2)),
            pltpu.SemaphoreType.DMA((3, 2)),
            pltpu.SemaphoreType.DMA((2, 4)),
            pltpu.SemaphoreType.DMA((2,)),
        ],
        compiler_params=pltpu.CompilerParams(collective_id=2, has_side_effects=True),
        name="scatter_terms",
    )(wants, glob, table, own, halo)


def attention_kernel(
    rand, ids, queries, d_out, selected, nearby, candidates,
    out, dq, table, own, halo, kv, near, glob, sems, gsems,
):
    seq, _, z, y, core = place()
    copies = [pltpu.make_async_copy(nearby.at[n], kv.at[n, pl.ds(0, 6)], gsems.at[n]) for n in (0, 1)]
    for e in range(4 * RAND):
        owner = rand[e // RAND, e % RAND] // 4
        away = (owner + core) % 2
        for n in (0, 1):
            row, slot = relation(z, y, owner, n)
            spot = ((away * 2 + n) * 8 + row) * 8 + slot
            copies.append(pltpu.make_async_copy(selected.at[spot], kv.at[n, 8 + e], sems.at[n, e]))
    for k in (0, 1):
        owner = ids[k] // 4
        away = (owner + core) % 2
        for n in (0, 1):
            row, slot = relation(z, y, owner, n)
            whole = (row < 3) | ((slot == 0) & (row < 7))
            parent = chosen(row, PARENT)
            parent = jnp.where((row == 7) & (slot >= 3) & (slot < 7), 1, parent)
            parent = jnp.where(whole, 0, parent)
            spot = ((away * 2 + n) * 3 + parent) * 2 + k
            copies.append(
                pltpu.make_async_copy(candidates.at[spot], kv.at[n, 6 + k], gsems.at[2 + 2 * n + k])
            )
    for copy in copies:
        copy.start()
    near[...] = jnp.zeros_like(near)
    glob[...] = jnp.zeros_like(glob)
    for n in (0, 1):
        table[n, NO_TERM:] = jnp.zeros((TERMS - NO_TERM, BLOCK, DH), BF16)
    for copy in copies:
        copy.wait()
    factor = DH ** (-0.5)
    dims = lambda a, b: (((a,), (b,)), ((), ()))

    def dot(a, b, at, bt):
        return lax.dot_general(a, b, dims(at, bt), preferred_element_type=F32)

    @pl.loop(0, 4)
    def _(i):
        rows = pl.ds(pl.multiple_of(i * BLOCK, BLOCK), BLOCK)
        stack = lambda ref: jnp.concatenate(
            [ref[rows, h * DH : (h + 1) * DH] for h in range(HEADS)], axis=0
        )
        q, g = stack(queries), stack(d_out)

        def listed(n):
            return jnp.concatenate(
                [
                    kv[n, pl.ds(i, 3)].reshape(3 * BLOCK, DH),
                    kv[n, 6:8].reshape(2 * BLOCK, DH),
                    kv[n, pl.ds(8 + i * RAND, RAND)].reshape(RAND * BLOCK, DH),
                ],
                axis=0,
            )

        k, v = listed(0), listed(1)
        scores = dot(k, q, 1, 1) * factor
        cut_first = jnp.logical_and(i == 0, seq == 0)
        cut_last = jnp.logical_and(i == 3, seq == lax.axis_size("seq") - 1)
        scores = jnp.concatenate(
            [
                jnp.where(cut_first, NEG_FILL, scores[:BLOCK]),
                scores[BLOCK : 2 * BLOCK],
                jnp.where(cut_last, NEG_FILL, scores[2 * BLOCK : 3 * BLOCK]),
                scores[3 * BLOCK :],
            ],
            axis=0,
        )
        peak = jnp.max(scores, axis=0, keepdims=True)
        weights = jnp.exp(scores - peak)
        probs = weights * (1.0 / jnp.sum(weights, axis=0, keepdims=True))
        probs16 = probs.astype(BF16)
        result = dot(v, probs16, 0, 0).astype(BF16)
        delta = jnp.sum(g.T.astype(F32) * result.astype(F32), axis=0, keepdims=True)
        dprobs = dot(v, g, 1, 1)
        dscores = (probs * (dprobs - delta)).astype(BF16)
        dquery = (dot(k, dscores, 0, 0) * factor).astype(BF16).T
        result = result.T
        for h in range(HEADS):
            out[rows, h * DH : (h + 1) * DH] = result[h * BLOCK : (h + 1) * BLOCK]
            dq[rows, h * DH : (h + 1) * DH] = dquery[h * BLOCK : (h + 1) * BLOCK]
        for n, terms in ((0, dot(dscores, q, 1, 0) * factor), (1, dot(probs16, g, 1, 0))):
            near[n, pl.ds(i, 3)] += terms[: 3 * BLOCK].reshape(3, BLOCK, DH)
            glob[n] += terms[3 * BLOCK : 5 * BLOCK].reshape(2, BLOCK, DH)
            table[n, pl.ds(i * RAND, RAND)] = terms[5 * BLOCK :].astype(BF16).reshape(RAND, BLOCK, DH)

    for n in (0, 1):
        own[n] = near[n, 1:5]
        halo[n, 0] = near[n, 0].astype(BF16)
        halo[n, 1] = near[n, 5].astype(BF16)
        for a in (0, 1):
            total = glob[n, a] + jnp.where(ids[0] == ids[1], glob[n, 1 - a], 0.0)
            table[n, 32 + a] = total.astype(BF16)


def attention(rand, ids, queries, d_out, selected, nearby, candidates):
    smem = pl.BlockSpec(memory_space=pltpu.SMEM)
    vmem = pl.BlockSpec(memory_space=pltpu.VMEM)
    tile = (BLOCK, DH)
    return pl.pallas_call(
        attention_kernel,
        out_shape=(
            jax.ShapeDtypeStruct(queries.shape, BF16),
            jax.ShapeDtypeStruct(queries.shape, BF16),
            jax.ShapeDtypeStruct((2, TERMS) + tile, BF16),
            jax.ShapeDtypeStruct((2, 4) + tile, F32),
            jax.ShapeDtypeStruct((2, 2) + tile, BF16),
        ),
        in_specs=[smem] * 2 + [vmem] * 2 + [pl.BlockSpec(memory_space=pl.ANY)] * 3,
        out_specs=(vmem,) * 5,
        scratch_shapes=[
            pltpu.VMEM((2, KV_ROWS) + tile, BF16),
            pltpu.VMEM((2, 6) + tile, F32),
            pltpu.VMEM((2, 2) + tile, F32),
            pltpu.SemaphoreType.DMA((2, 4 * RAND)),
            pltpu.SemaphoreType.DMA((6,)),
        ],
        compiler_params=pltpu.CompilerParams(vmem_limit_bytes=60 * 1024 * 1024),
        name="block_attention",
    )(rand, ids, queries, d_out, selected, nearby, candidates)


def copy_kernel(a, b, x, y):
    x[...] = a[...]
    y[...] = b[...]


def body(queries, keys, values, d_out, rand_blocks, glob_blocks):
    selected, nearby, candidates, wants = gather_all(keys, values, rand_blocks, glob_blocks)
    out, dq, table, own, halo = attention(
        rand_blocks,
        glob_blocks,
        queries,
        d_out,
        selected.reshape(256, BLOCK, DH),
        nearby,
        candidates.reshape(24, BLOCK, DH),
    )
    dk, dv = scatter_all(wants, glob_blocks, table, own, halo)
    dk, dv = pl.pallas_call(
        copy_kernel, out_shape=[jax.ShapeDtypeStruct(dk.shape, dk.dtype)] * 2, name="write_out"
    )(dk, dv)
    return (out, dq, dk, dv)


def solution(mesh):
    in_specs = (
        P("seq", "head"),
        P(("seq", "head"), None),
        P(("seq", "head"), None),
        P("seq", "head"),
        P("seq", None),
        P(),
    )
    out_specs = (
        P("seq", "head"),
        P("seq", "head"),
        P(("seq", "head"), None),
        P(("seq", "head"), None),
    )
    return jax.shard_map(body, mesh=mesh, in_specs=in_specs, out_specs=out_specs, check_vma=False)
```

```python
import jax
import jax.numpy as jnp
from jax import lax
from jax.experimental import pallas as pl
from jax.experimental.pallas import tpu as pltpu
from jax.sharding import PartitionSpec as P

DH = 128
KVH = 4
HEADS = 8
BLOCK = 64
RAND = 8
PAIR = 2 * DH
RING = 8
NEG_FILL = -1e30
BF16 = jnp.bfloat16
F32 = jnp.float32
MESH = pl.DeviceIdType.MESH

ORDER = (0, 1, -1, 2, -2, 3, -3, 4)
SLOT = {d: i for i, d in enumerate(ORDER)}
ROWS = (0, 3, -3, 1, -1, 2, -2, 4)
PATH = {1: 24, -1: 25, 2: 26, -2: 27}
CHUNKS = 28
INNER = ((1, 3), (3, 5), (5, 7), (7, 8))
LEAVES = (
    (1, 1, 7, ((0, 3), (7, 8))),
    (2, -1, 7, ((3, 5), (5, 7))),
    (1, -1, 5, INNER),
    (2, 1, 6, INNER),
    (0, 1, 3, INNER),
    (0, -1, 4, INNER),
)
SIDES = {("z", 1): 0, ("z", -1): 1, ("y", 1): 2, ("y", -1): 3}
CHUNK_US = 1.78
HALF_US = 0.05
HOP_US = 2.8
TABLE_US = 3.0
MARGIN_US = 3.0
KV_ROWS = 40
PARTS = 1
TERMS = 36
NO_TERM = 34
WANT = (1, 2 * RING * RING)


def axis_of(half, major):
    return "zy"[half] if major else "yz"[half]


def ordered(tasks):
    followers = {}
    for task in tasks:
        for dep in task[3]:
            followers.setdefault(dep, []).append(task)
    left = {}

    def remaining(task):
        if task[0] not in left:
            after = max((remaining(t) for t in followers.get(task[0], ())), default=0.0)
            left[task[0]] = task[2] + HOP_US + after
        return left[task[0]]

    arrival, free, result = {}, {}, []
    waiting = list(tasks)
    while waiting:
        best = None
        for task in waiting:
            if all(dep in arrival for dep in task[3]):
                ready = max([arrival[dep] for dep in task[3]], default=0.0)
                key = (max(ready, free.get(task[1], 0.0)), -remaining(task))
                if best is None or key < best[0]:
                    best = (key, task)
        (start, _), task = best
        waiting.remove(task)
        name, link, time, deps = task
        free[link] = start + time
        arrival[name] = start + time + HOP_US
        result.append((start, task))
    return result, arrival


def far_sign(half, row):
    return 1 if (half + row) % 2 == 0 else -1


def gather_tasks():
    tasks = []
    for half in (0, 1):
        minor, major = axis_of(half, False), axis_of(half, True)
        whole = {}
        for step in range(3):
            for sign in (1, -1):
                name = ("H", half, sign, step)
                deps = (("H", half, sign, step - 1),) if step else ()
                tasks.append((name, (major, sign), CHUNK_US, deps))
                if step < 2:
                    whole[PATH[sign * (step + 1)]] = name
                else:
                    whole[8 if sign > 0 else 16] = name
        for row in range(3):
            far = far_sign(half, row)
            for sign in (1, -1):
                for step in range(4 if sign == far else 3):
                    name = ("m", half, row, sign, step)
                    if step:
                        deps = (("m", half, row, sign, step - 1),)
                    else:
                        deps = (whole[8 * row],) if row else ()
                    tasks.append((name, (minor, sign), CHUNK_US, deps))
                    to = 7 if step == 3 else SLOT[sign * (step + 1)]
                    whole[8 * row + to] = name
        for row, sign, to, ranges in LEAVES:
            for lo, hi in ranges:
                deps = tuple(whole[8 * row + s] for s in range(lo, hi) if row or s)
                for r in (0, 1):
                    name = ("L", half, row, sign, to, lo, hi, r)
                    tasks.append((name, (major, sign), CHUNK_US * (hi - lo) / 4, deps))
        copies = tuple(whole.values())
        for sign in (1, -1):
            tasks.append((("G", half, sign), (major, sign), CHUNK_US / 2, copies))
        for sign in (1, -1):
            tasks.append((("X", half, sign), "p", HALF_US, (("G", half, sign),)))
        for row in range(8):
            groups = ((0, 5), (5, 8)) if row < 3 else ((0, 1),) if row < 7 else ()
            for lo, hi in groups:
                if row < 3:
                    deps = tuple(whole[8 * row + s] for s in range(lo, hi) if row or s)
                else:
                    deps = (whole[PATH[ROWS[row]]],)
                tasks.append((("P", half, row, lo, hi), "p", HALF_US * (hi - lo), deps))
    late = [task for _, task in ordered(tasks)[0] if task[0][0] in "PX"]
    main, arrival = ordered([task for task in tasks if task[0][0] not in "PX"])
    result, seen = [], set()
    for start, task in main:
        for other in [t for t in late if t[0][0] == "P"]:
            if set(other[3]) <= seen or max(arrival[d] for d in other[3]) + MARGIN_US < start:
                late.remove(other)
                result.append(other)
                seen.update(other[3])
        result.append(task)
        seen.update(task[3])
    return result + late


def children(row, slot):
    if row == 0:
        return [(3, 1), (4, -1)] if slot else []
    result = []
    if slot:
        result.append((5, -1) if row == 1 else (6, 1))
    if row == 1 and slot in (0, 1, 2, 7):
        result.append((7, 1))
    if row == 2 and slot in (3, 4, 5, 6):
        result.append((7, -1))
    return result


def scatter_tasks():
    tasks = [(("T", 0), "p", TABLE_US, ())]
    for half in (0, 1):
        major = axis_of(half, True)
        for sign in (1, -1):
            tasks.append((("G", half, sign), (major, sign), CHUNK_US / 2, (("T", 0),)))
    leaf = {}
    for row, sign, to, ranges in LEAVES:
        for lo, hi in reversed(ranges):
            for half in (0, 1):
                major = axis_of(half, True)
                for r in (0, 1):
                    name = ("L", half, to, sign, lo, hi, r)
                    tasks.append((name, (major, -sign), CHUNK_US * (hi - lo) / 4, ()))
                    for s in range(lo, hi):
                        leaf[half, to, s, r] = name
    for half in (0, 1):
        minor, major = axis_of(half, False), axis_of(half, True)
        extra = (("G", half, 1), ("G", half, -1))

        def leaves(row, slot):
            return tuple(leaf[half, to, slot, r] for to, _ in children(row, slot) for r in (0, 1)) + extra

        for row in (1, 2, 0):
            for sign in (1, -1):
                top = 4 if sign == far_sign(half, row) else 3
                for step in range(top, 0, -1):
                    deps = leaves(row, 7 if step == 4 else SLOT[sign * step])
                    if step < top:
                        deps += (("m", half, row, sign, step + 1),)
                    tasks.append((("m", half, row, sign, step), (minor, -sign), CHUNK_US, deps))
        for sign in (1, -1):
            row = 1 if sign > 0 else 2
            for step in (3, 2, 1):
                if step == 3:
                    deps = leaves(row, 0) + (("m", half, row, 1, 1), ("m", half, row, -1, 1))
                else:
                    deps = (("H", half, sign, step + 1),)
                tasks.append((("H", half, sign, step), (major, -sign), CHUNK_US, deps))
        deps = tuple((k, half, s, 1) for k in "H" for s in (1, -1))
        deps += (("m", half, 0, 1, 1), ("m", half, 0, -1, 1))
        tasks.append((("F", half), ("f", half), 0.0, deps))
    return [task for _, task in ordered(tasks)[0]]


GATHER = gather_tasks()
SCATTER = scatter_tasks()
GATHER_SENDS = {task[0]: i for i, task in enumerate(GATHER)}
SCATTER_SENDS = {t[0]: i for i, t in enumerate(t for t in SCATTER if t[0][0] != "F")}


def place():
    seq = lax.axis_index("seq")
    head = lax.axis_index("head")
    return seq, head, seq // 16, (seq // 2) % RING, seq % 2


def neighbours(seq, head, z, y, core):
    up = lambda v: lax.rem(v + 1, RING)
    down = lambda v: lax.rem(v + RING - 1, RING)
    index = lambda zz, yy, cc: zz * 16 + yy * 2 + cc
    count = 2 * RING * RING
    peers = {}
    for name, cc in ((0, core), (1, 1 - core)):
        peers["z", 1, name] = index(up(z), y, cc)
        peers["z", -1, name] = index(down(z), y, cc)
        peers["y", 1, name] = index(z, up(y), cc)
        peers["y", -1, name] = index(z, down(y), cc)
    peers["p"] = index(z, y, 1 - core)
    peers["next"] = lax.rem(seq + 1, count)
    peers["last"] = lax.rem(seq + count - 1, count)
    return {k: {"seq": v, "head": head} for k, v in peers.items()}


def enter(peers, seq, head):
    barrier = pltpu.get_barrier_semaphore()
    everyone = list(peers.values())
    everyone += [{"seq": seq, "head": lax.rem(head + j, KVH)} for j in (1, 2, 3)]
    for peer in everyone:
        pl.semaphore_signal(barrier, inc=1, device_id=peer, device_id_type=MESH)
    pl.semaphore_wait(barrier, len(everyone))


def remote(src, dst, send, recv, peer):
    return pltpu.make_async_remote_copy(
        src_ref=src,
        dst_ref=dst,
        send_sem=send,
        recv_sem=recv,
        device_id=peer,
        device_id_type=MESH,
    )


def owner_of(half, z, y, core, far, near):
    dz, dy = (far, near) if half == 0 else (near, far)
    return lax.rem(z - dz + RING, RING) * 16 + lax.rem(y - dy + RING, RING) * 2 + core


def chunk_offsets(chunk):
    if chunk < 24:
        return ROWS[chunk // 8], ORDER[chunk % 8]
    return (1, -1, 2, -2)[chunk - 24], 0


def chosen(value, table):
    result = table[0]
    for i, entry in enumerate(table[1:], 1):
        result = jnp.where(value == i, entry, result)
    return result


SLOTS_MOD = [SLOT[d] if d <= 4 else SLOT[d - RING] for d in range(RING)]
ROWS_MOD = [ROWS.index(d) if d <= 4 else ROWS.index(d - RING) for d in range(RING)]
SLOTS_PACKED = sum(v << (3 * d) for d, v in enumerate(SLOTS_MOD))
ROWS_PACKED = sum(v << (3 * d) for d, v in enumerate(ROWS_MOD))
PARENT = [0, 0, 0, 2, 1, 1, 2, 2]


def relation(z, y, owner, half):
    dz = (z + RING - owner // 16) % RING
    dy = (y + RING - (owner // 2) % RING) % RING
    far, near = (dz, dy) if half == 0 else (dy, dz)
    return chosen(far, ROWS_MOD), chosen(near, SLOTS_MOD)


def gather_kernel(
    keys, values, rand, glob, sel_out, near_out, cand_out, wants, want,
    full0, full1, picked, staged, extra, scal, send, recv, xsend, xrecv, osend, orecv, lsem, csem,
):
    seq, head, z, y, core = place()
    peers = neighbours(seq, head, z, y, core)
    full = (full0, full1)
    lane = lax.broadcasted_iota(jnp.int32, (1, 2 * RING * RING), 1)
    named = jnp.full_like(lane, 4 * NO_TERM)
    for e in range(4 * RAND):
        block = rand[e // RAND, e % RAND]
        named = jnp.where(lane == block // 4, 4 * e + block % 4, named)
    want[...] = named
    local = pltpu.make_async_copy(want, wants.at[8], lsem.at[0])
    local.start()
    local.wait()
    enter(peers, seq, head)
    pieces = (keys, values)
    xcopies = []
    for j in (1, 2, 3):
        to = lax.rem(head + j, KVH)
        for n, source in enumerate(pieces):
            xcopies.append(
                remote(
                    source.at[:, pl.ds(pl.multiple_of(to * DH, DH), DH)],
                    full[n].at[0, head],
                    xsend.at[j - 1, n],
                    xrecv.at[j - 1, n],
                    {"seq": seq, "head": to},
                )
            )
            xcopies[-1].start()
    ocopies = [remote(wants.at[8], wants.at[9], osend.at[0], orecv.at[0], peers["p"])]
    for (axis, sign), side in SIDES.items():
        back = SIDES[axis, -sign] * 2
        for r in (0, 1):
            i = len(ocopies)
            peer = peers[axis, sign, r]
            ocopies.append(remote(wants.at[8], wants.at[back + r], osend.at[i], orecv.at[i], peer))
    for copy in ocopies:
        copy.start()
    local = []
    for n, source in enumerate(pieces):
        mine = source.at[:, pl.ds(pl.multiple_of(head * DH, DH), DH)]
        local.append(pltpu.make_async_copy(mine, full[n].at[0, head], lsem.at[1 + n]))
    for copy in local:
        copy.start()
    for copy in local:
        copy.wait()
    for copy in xcopies:
        copy.wait_recv()

    started = {}
    waited = set()
    tail = []

    def wait_for(deps):
        for dep in deps:
            if dep not in waited:
                waited.add(dep)
                started[dep].wait_recv()

    def finish_start():
        for copy in ocopies:
            copy.wait_recv()
        scalars = pltpu.make_async_copy(wants, scal, lsem.at[0])
        scalars.start()
        for half in (0, 1):
            i = 10 + 2 * half
            tail.append(remote(full[half].at[0, 3], near_out.at[half, 0], osend.at[i], orecv.at[i], peers["next"]))
            tail.append(
                remote(full[half].at[0, 0], near_out.at[half, 5], osend.at[i + 1], orecv.at[i + 1], peers["last"])
            )
            tail.append(
                pltpu.make_async_copy(full[half].at[0], near_out.at[half, pl.ds(1, 4)], lsem.at[1 + half])
            )
        for copy in tail:
            copy.start()
        scalars.wait()

    def pick(half, chunk, side):
        far, near = chunk_offsets(chunk)
        inner = scal[side, 0, owner_of(half, z, y, core, far, near)] % 4
        block = full[half][chunk, 0]
        for b in (1, 2, 3):
            block = jnp.where(inner == b, full[half][chunk, b], block)
        return block

    ready = False
    passed = set()
    locals_ = []
    for name, link, _, deps in GATHER:
        wait_for(deps)
        kind, half = name[:2]
        major = axis_of(half, True)
        if kind in "LP" and not ready:
            finish_start()
            ready = True
        i = GATHER_SENDS[name]
        peer = peers["p"] if link == "p" else peers[link[0], link[1], 0]
        extra_sends = []
        if kind == "H":
            _, _, sign, step = name
            src = full[half].at[PATH[sign * step] if step else 0]
            dst = full[half].at[PATH[sign * (step + 1)] if step < 2 else (8 if sign > 0 else 16)]
        elif kind == "m":
            _, _, row, sign, step = name
            src = full[half].at[8 * row + SLOT[sign * step]]
            dst = full[half].at[8 * row + (7 if step == 3 else SLOT[sign * (step + 1)])]
        elif kind == "L":
            _, _, row, sign, to, lo, hi, r = name
            side = SIDES[major, sign] * 2
            for s in range(lo, hi):
                staged[half, r, to, s] = pick(half, 8 * row + s, side + r)
            src = staged.at[half, r, to, pl.ds(lo, hi - lo)]
            dst = sel_out.at[r, half, to, pl.ds(lo, hi - lo)]
            peer = peers[major, sign, r]
        elif kind == "P":
            _, _, row, lo, hi = name
            for s in range(lo, hi):
                chunk = 8 * row + s if row < 3 else PATH[ROWS[row]] if row < 7 and s == 0 else None
                if chunk is not None:
                    for r in (0, 1):
                        picked[half, r, row, s] = pick(half, chunk, 8 + r)
            span = pl.ds(lo, hi - lo)
            src = picked.at[half, 1, row, span]
            dst = sel_out.at[1, half, row, span]
            keep = pltpu.make_async_copy(
                picked.at[half, 0, row, span], sel_out.at[0, half, row, span], csem.at[len(locals_)]
            )
            keep.start()
            locals_.append(keep)
        elif kind == "G":
            sign = name[2]
            if half not in passed:
                passed.add(half)
                for k in (0, 1):
                    row, slot = relation(z, y, glob[k] // 4, half)
                    chunk = jnp.where(row < 3, row * 8 + slot, jnp.where(row < 7, 21 + row, 0))
                    extra[half, k] = full[half][chunk, glob[k] % 4]
                keep = pltpu.make_async_copy(extra.at[half], cand_out.at[0, half, 0], csem.at[len(locals_)])
                keep.start()
                locals_.append(keep)
                j = 14 + half
                tail.append(
                    remote(extra.at[half], cand_out.at[1, half, 0], osend.at[j], orecv.at[j], peers["p"])
                )
                tail[-1].start()
            src = extra.at[half]
            dst = cand_out.at[0, half, 2 if sign > 0 else 1]
        else:
            sign = name[2]
            at = 2 if sign > 0 else 1
            src = cand_out.at[0, half, at]
            dst = cand_out.at[1, half, at]
        copy = remote(src, dst, send.at[i], recv.at[i], peer)
        copy.start()
        started[name] = copy
    wait_for(started)
    for copy in xcopies + ocopies + list(started.values()):
        copy.wait_send()
    for copy in tail + locals_:
        copy.wait()


def gather_all(keys, values, rand, glob):
    count = len(GATHER)
    keeps = 2 + sum(task[0][0] == "P" for task in GATHER)
    hbm = pl.BlockSpec(memory_space=pl.ANY)
    vmem = pl.BlockSpec(memory_space=pltpu.VMEM)
    smem = pl.BlockSpec(memory_space=pltpu.SMEM)
    return pl.pallas_call(
        gather_kernel,
        out_shape=(
            jax.ShapeDtypeStruct((2, 2, 8, 8, BLOCK, DH), BF16),
            jax.ShapeDtypeStruct((2, 6, BLOCK, DH), BF16),
            jax.ShapeDtypeStruct((2, 2, 3, 2, BLOCK, DH), BF16),
            jax.ShapeDtypeStruct((10,) + WANT, jnp.int32),
        ),
        in_specs=[vmem] * 2 + [smem] * 2,
        out_specs=(hbm, hbm, hbm, vmem),
        scratch_shapes=[
            pltpu.VMEM(WANT, jnp.int32),
            pltpu.VMEM((CHUNKS, 4, BLOCK, DH), BF16),
            pltpu.VMEM((CHUNKS, 4, BLOCK, DH), BF16),
            pltpu.VMEM((2, 2, 8, 8, BLOCK, DH), BF16),
            pltpu.VMEM((2, 2, 8, 8, BLOCK, DH), BF16),
            pltpu.VMEM((2, 2, BLOCK, DH), BF16),
            pltpu.SMEM((10,) + WANT, jnp.int32),
            pltpu.SemaphoreType.DMA((count,)),
            pltpu.SemaphoreType.DMA((count,)),
            pltpu.SemaphoreType.DMA((3, 2)),
            pltpu.SemaphoreType.DMA((3, 2)),
            pltpu.SemaphoreType.DMA((16,)),
            pltpu.SemaphoreType.DMA((16,)),
            pltpu.SemaphoreType.DMA((3,)),
            pltpu.SemaphoreType.DMA((keeps,)),
        ],
        compiler_params=pltpu.CompilerParams(collective_id=1, has_side_effects=True),
        name="gather_blocks",
    )(keys, values, rand, glob)


def scatter_kernel(
    wants, glob, table, own, halo, dk, dv,
    mirror, staged, landed, line, origin, path, stem, gsum, gin, extra, rim, final,
    send, recv, xsend, xrecv, hsem, lsem,
):
    seq, head, z, y, core = place()
    peers = neighbours(seq, head, z, y, core)
    enter(peers, seq, head)
    first = []
    for half in (0, 1):
        i = 2 * half
        first.append(remote(halo.at[half, 0], rim.at[half, 1], hsem.at[0, i], hsem.at[1, i], peers["last"]))
        first.append(
            remote(halo.at[half, 1], rim.at[half, 0], hsem.at[0, i + 1], hsem.at[1, i + 1], peers["next"])
        )
    started = {}
    waited = set()
    ready = set()
    passed = set()

    def block_sum(half, chunk, sides, b):
        far, near = chunk_offsets(chunk)
        owner = owner_of(half, z, y, core, far, near)
        mine, theirs = wants[8, 0, owner], wants[9, 0, owner]
        total = jnp.where(mine % 4 == b, table[half, mine // 4].astype(F32), 0.0)
        total += jnp.where(theirs % 4 == b, mirror[half, theirs // 4].astype(F32), 0.0)
        kind = sum(1 if sign > 0 else 2 for _, sign in sides)
        number = owner * 4 + b
        total += jnp.where(
            number == glob[0],
            extra[half, kind, 0],
            jnp.where(number == glob[1], extra[half, kind, 1], 0.0),
        )
        major = axis_of(half, True)
        for to, sign in sides:
            for r in (0, 1):
                inner = wants[SIDES[major, sign] * 2 + r, 0, owner] % 4
                term = landed[half, r, to, chunk % 8].astype(F32)
                total += jnp.where(inner == b, term, 0.0)
        return total

    for name, link, _, deps in SCATTER:
        for dep in deps:
            if dep not in waited:
                waited.add(dep)
                started[dep].wait_recv()
        kind, half = name[:2]
        if kind in "mHF" and half not in ready:
            ready.add(half)
            for k in (0, 1):
                alone = table[half, 32 + k].astype(F32) + mirror[half, 32 + k].astype(F32)
                up, down = gin[half, 0, k].astype(F32), gin[half, 1, k].astype(F32)
                extra[half, 0, k] = alone
                extra[half, 1, k] = alone + up
                extra[half, 2, k] = alone + down
                extra[half, 3, k] = alone + up + down
        if kind == "F":
            for copy in first[2 * half : 2 * half + 2]:
                copy.wait_recv()

            for b in range(4):
                total = block_sum(half, 0, [], b) + own[half, b]
                total += line[half, 0, 0, b].astype(F32) + origin[half, 0, b].astype(F32)
                total += stem[half, 0, b].astype(F32) + stem[half, 1, b].astype(F32)
                if b in (0, 3):
                    total += rim[half, b // 3].astype(F32)
                final[half, b] = total.astype(BF16)
            continue
        if kind == "T":
            src, dst = table, mirror
        elif kind == "G":
            if half not in passed:
                passed.add(half)
                for k in (0, 1):
                    alone = table[half, 32 + k].astype(F32) + mirror[half, 32 + k].astype(F32)
                    gsum[half, k] = alone.astype(BF16)
            src, dst = gsum.at[half], gin.at[half, 1 if name[2] > 0 else 0]
        elif kind == "L":
            _, _, to, sign, lo, hi, r = name
            for s in range(lo, hi):
                owner = owner_of(half, z, y, 1 - core if r else core, ROWS[to], ORDER[s])
                staged[half, r, to, s] = table[half, wants[8, 0, owner] // 4]
            span = pl.ds(lo, hi - lo)
            src, dst = staged.at[half, r, to, span], landed.at[half, r, to, span]
        elif kind == "m":
            _, _, row, sign, step = name
            slot = 7 if step == 4 else SLOT[sign * step]
            arrived = any(dep[0] == "m" for dep in deps)
            sides = children(row, slot)

            @pl.loop(0, 4)
            def _(b):
                total = block_sum(half, 8 * row + slot, sides, b)
                if arrived:
                    total += line[half, row, slot, b].astype(F32)
                line[half, row, slot, b] = total.astype(BF16)

            src = line.at[half, row, slot]
            if step > 1:
                dst = line.at[half, row, SLOT[sign * (step - 1)]]
            else:
                dst = line.at[half, row, 0] if sign > 0 else origin.at[half, row]
        else:
            _, _, sign, step = name
            if step == 3:
                row = 1 if sign > 0 else 2
                sides = children(row, 0)

                @pl.loop(0, 4)
                def _(b):
                    total = block_sum(half, 8 * row, sides, b)
                    total += line[half, row, 0, b].astype(F32) + origin[half, row, b].astype(F32)
                    line[half, row, 0, b] = total.astype(BF16)

                src = line.at[half, row, 0]
            else:
                chunk = PATH[sign * step]

                @pl.loop(0, 4)
                def _(b):
                    total = block_sum(half, chunk, [], b) + path[half, chunk - 24, b].astype(F32)
                    path[half, chunk - 24, b] = total.astype(BF16)

                src = path.at[half, chunk - 24]
            if step > 1:
                dst = path.at[half, PATH[sign * (step - 1)] - 24]
            else:
                dst = stem.at[half, 0 if sign > 0 else 1]
        i = SCATTER_SENDS[name]
        peer = peers["p"] if link == "p" else peers[link[0], link[1], name[6] if kind == "L" else 0]
        copy = remote(src, dst, send.at[i], recv.at[i], peer)
        copy.start()
        started[name] = copy
        if kind == "T":
            for copy in first:
                copy.start()

    here = pl.ds(pl.multiple_of(head * DH, DH), DH)
    copies = []
    for j in (1, 2, 3):
        to = lax.rem(head + j, KVH)
        for n, target in enumerate((dk, dv)):
            copies.append(
                remote(
                    final.at[n, to],
                    target.at[:, here],
                    xsend.at[j - 1, n],
                    xrecv.at[j - 1, n],
                    {"seq": seq, "head": to},
                )
            )
            copies[-1].start()
    for n, target in enumerate((dk, dv)):
        copies.append(pltpu.make_async_copy(final.at[n, head], target.at[:, here], lsem.at[n]))
        copies[-1].start()
    for copy in copies:
        copy.wait()
    for copy in first + list(started.values()):
        copy.wait_send()


def scatter_all(wants, glob, table, own, halo):
    count = len(SCATTER_SENDS)
    vmem = pl.BlockSpec(memory_space=pltpu.VMEM)
    smem = pl.BlockSpec(memory_space=pltpu.SMEM)
    tile = (BLOCK, DH)
    return pl.pallas_call(
        scatter_kernel,
        out_shape=(jax.ShapeDtypeStruct((BLOCK, KVH * DH), BF16),) * 2,
        in_specs=[smem] * 2 + [vmem] * 3,
        out_specs=(pl.BlockSpec(memory_space=pl.ANY),) * 2,
        scratch_shapes=[
            pltpu.VMEM((2, TERMS) + tile, BF16),
            pltpu.VMEM((2, 2, 8, 8) + tile, BF16),
            pltpu.VMEM((2, 2, 8, 8) + tile, BF16),
            pltpu.VMEM((2, 3, 8, 4) + tile, BF16),
            pltpu.VMEM((2, 3, 4) + tile, BF16),
            pltpu.VMEM((2, 4, 4) + tile, BF16),
            pltpu.VMEM((2, 2, 4) + tile, BF16),
            pltpu.VMEM((2, 2) + tile, BF16),
            pltpu.VMEM((2, 2, 2) + tile, BF16),
            pltpu.VMEM((2, 4, 2) + tile, F32),
            pltpu.VMEM((2, 2) + tile, BF16),
            pltpu.VMEM((2, 4) + tile, BF16),
            pltpu.SemaphoreType.DMA((count,)),
            pltpu.SemaphoreType.DMA((count,)),
            pltpu.SemaphoreType.DMA((3, 2)),
            pltpu.SemaphoreType.DMA((3, 2)),
            pltpu.SemaphoreType.DMA((2, 4)),
            pltpu.SemaphoreType.DMA((2,)),
        ],
        compiler_params=pltpu.CompilerParams(collective_id=2, has_side_effects=True),
        name="scatter_terms",
    )(wants, glob, table, own, halo)


def attention_kernel(
    rand, ids, queries, d_out, selected, nearby, candidates,
    out, dq, table, own, halo, kv, near, glob, sems, gsems,
):
    seq, _, z, y, core = place()
    copies = [pltpu.make_async_copy(nearby.at[n], kv.at[n, pl.ds(0, 6)], gsems.at[n]) for n in (0, 1)]
    for copy in copies:
        copy.start()

    def fetch(n, e, spot):
        return pltpu.make_async_copy(selected.at[spot], kv.at[n, 8 + e], sems.at[n, e])

    for k in (0, 1):
        owner = ids[k] // 4
        away = (owner + core) % 2
        for n in (0, 1):
            row, slot = relation(z, y, owner, n)
            whole = (row < 3) | ((slot == 0) & (row < 7))
            parent = chosen(row, PARENT)
            parent = jnp.where((row == 7) & (slot >= 3) & (slot < 7), 1, parent)
            parent = jnp.where(whole, 0, parent)
            spot = ((away * 2 + n) * 3 + parent) * 2 + k
            copies.append(
                pltpu.make_async_copy(candidates.at[spot], kv.at[n, 6 + k], gsems.at[2 + 2 * n + k])
            )
            copies[-1].start()
    def start_fetches(i, e):
        owner = rand[i, e] // 4
        away = (owner + core) % 2
        dz = 3 * ((z + RING - owner // 16) % RING)
        dy = 3 * ((y + RING - (owner // 2) % RING) % RING)
        for n, far, near_by in ((0, dz, dy), (1, dy, dz)):
            at = ((ROWS_PACKED >> far) & 7) * 8 + ((SLOTS_PACKED >> near_by) & 7)
            fetch(n, i * RAND + e, (away * 2 + n) * 64 + at).start()

    for e in range(RAND):
        start_fetches(0, e)
    near[...] = jnp.zeros_like(near)
    glob[...] = jnp.zeros_like(glob)
    for n in (0, 1):
        table[n, NO_TERM:] = jnp.zeros((TERMS - NO_TERM, BLOCK, DH), BF16)
    for copy in copies:
        copy.wait()
    factor = DH ** (-0.5)
    dims = lambda a, b: (((a,), (b,)), ((), ()))

    def dot(a, b, at, bt):
        return lax.dot_general(a, b, dims(at, bt), preferred_element_type=F32)

    for i in range(4):
        for e in range(RAND):
            for n in (0, 1):
                fetch(n, i * RAND + e, 0).wait()
            if i < 3:
                start_fetches(i + 1, e)
        rows = pl.ds(i * BLOCK, BLOCK)
        def listed(n):
            return jnp.concatenate(
                [
                    kv[n, pl.ds(i, 3)].reshape(3 * BLOCK, DH),
                    kv[n, 6:8].reshape(2 * BLOCK, DH),
                    kv[n, pl.ds(8 + i * RAND, RAND)].reshape(RAND * BLOCK, DH),
                ],
                axis=0,
            )

        k, v = listed(0), listed(1)
        cut_first = jnp.logical_and(i == 0, seq == 0)
        cut_last = jnp.logical_and(i == 3, seq == lax.axis_size("seq") - 1)
        sums = [None, None]
        for part in range(PARTS):
            heads = range(part * HEADS // PARTS, (part + 1) * HEADS // PARTS)
            stack = lambda ref: jnp.concatenate([ref[rows, h * DH : (h + 1) * DH] for h in heads], axis=0)
            q, g = stack(queries), stack(d_out)
            scores = dot(k, q, 1, 1) * factor
            scores = jnp.concatenate(
                [
                    jnp.where(cut_first, NEG_FILL, scores[:BLOCK]),
                    scores[BLOCK : 2 * BLOCK],
                    jnp.where(cut_last, NEG_FILL, scores[2 * BLOCK : 3 * BLOCK]),
                    scores[3 * BLOCK :],
                ],
                axis=0,
            )
            peak = jnp.max(scores, axis=0, keepdims=True)
            weights = jnp.exp(scores - peak)
            probs = weights * (1.0 / jnp.sum(weights, axis=0, keepdims=True))
            probs16 = probs.astype(BF16)
            result = dot(v, probs16, 0, 0).astype(BF16)
            delta = jnp.sum(g.T.astype(F32) * result.astype(F32), axis=0, keepdims=True)
            dprobs = dot(v, g, 1, 1)
            dscores = (probs * (dprobs - delta)).astype(BF16)
            dquery = (dot(k, dscores, 0, 0) * factor).astype(BF16).T
            result = result.T
            for n, h in enumerate(heads):
                out[rows, h * DH : (h + 1) * DH] = result[n * BLOCK : (n + 1) * BLOCK]
                dq[rows, h * DH : (h + 1) * DH] = dquery[n * BLOCK : (n + 1) * BLOCK]
            for n, terms in ((0, dot(dscores, q, 1, 0)), (1, dot(probs16, g, 1, 0))):
                sums[n] = terms if sums[n] is None else sums[n] + terms
        for n, terms in ((0, sums[0] * factor), (1, sums[1])):
            near[n, pl.ds(i, 3)] += terms[: 3 * BLOCK].reshape(3, BLOCK, DH)
            glob[n] += terms[3 * BLOCK : 5 * BLOCK].reshape(2, BLOCK, DH)
            table[n, pl.ds(i * RAND, RAND)] = terms[5 * BLOCK :].astype(BF16).reshape(RAND, BLOCK, DH)

    for n in (0, 1):
        own[n] = near[n, 1:5]
        halo[n, 0] = near[n, 0].astype(BF16)
        halo[n, 1] = near[n, 5].astype(BF16)
        for a in (0, 1):
            total = glob[n, a] + jnp.where(ids[0] == ids[1], glob[n, 1 - a], 0.0)
            table[n, 32 + a] = total.astype(BF16)


def attention(rand, ids, queries, d_out, selected, nearby, candidates):
    smem = pl.BlockSpec(memory_space=pltpu.SMEM)
    vmem = pl.BlockSpec(memory_space=pltpu.VMEM)
    tile = (BLOCK, DH)
    return pl.pallas_call(
        attention_kernel,
        out_shape=(
            jax.ShapeDtypeStruct(queries.shape, BF16),
            jax.ShapeDtypeStruct(queries.shape, BF16),
            jax.ShapeDtypeStruct((2, TERMS) + tile, BF16),
            jax.ShapeDtypeStruct((2, 4) + tile, F32),
            jax.ShapeDtypeStruct((2, 2) + tile, BF16),
        ),
        in_specs=[smem] * 2 + [vmem] * 2 + [pl.BlockSpec(memory_space=pl.ANY)] * 3,
        out_specs=(vmem,) * 5,
        scratch_shapes=[
            pltpu.VMEM((2, KV_ROWS) + tile, BF16),
            pltpu.VMEM((2, 6) + tile, F32),
            pltpu.VMEM((2, 2) + tile, F32),
            pltpu.SemaphoreType.DMA((2, 4 * RAND)),
            pltpu.SemaphoreType.DMA((6,)),
        ],
        compiler_params=pltpu.CompilerParams(vmem_limit_bytes=60 * 1024 * 1024),
        name="block_attention",
    )(rand, ids, queries, d_out, selected, nearby, candidates)


def copy_kernel(a, b, x, y):
    x[...] = a[...]
    y[...] = b[...]


def body(queries, keys, values, d_out, rand_blocks, glob_blocks):
    selected, nearby, candidates, wants = gather_all(keys, values, rand_blocks, glob_blocks)
    out, dq, table, own, halo = attention(
        rand_blocks,
        glob_blocks,
        queries,
        d_out,
        selected.reshape(256, BLOCK, DH),
        nearby,
        candidates.reshape(24, BLOCK, DH),
    )
    dk, dv = scatter_all(wants, glob_blocks, table, own, halo)
    dk, dv = pl.pallas_call(
        copy_kernel, out_shape=[jax.ShapeDtypeStruct(dk.shape, dk.dtype)] * 2, name="write_out"
    )(dk, dv)
    return (out, dq, dk, dv)


def solution(mesh):
    in_specs = (
        P("seq", "head"),
        P(("seq", "head"), None),
        P(("seq", "head"), None),
        P("seq", "head"),
        P("seq", None),
        P(),
    )
    out_specs = (
        P("seq", "head"),
        P("seq", "head"),
        P(("seq", "head"), None),
        P(("seq", "head"), None),
    )
    return jax.shard_map(body, mesh=mesh, in_specs=in_specs, out_specs=out_specs, check_vma=False)
```

```python
import jax
import jax.numpy as jnp
from jax import lax
from jax.experimental import pallas as pl
from jax.experimental.pallas import tpu as pltpu
from jax.sharding import PartitionSpec as P

DH = 128
KVH = 4
HEADS = 8
BLOCK = 64
RAND = 8
PAIR = 2 * DH
RING = 8
NEG_FILL = -1e30
BF16 = jnp.bfloat16
F32 = jnp.float32
MESH = pl.DeviceIdType.MESH

ORDER = (0, 1, -1, 2, -2, 3, -3, 4)
SLOT = {d: i for i, d in enumerate(ORDER)}
ROWS = (0, 3, -3, 1, -1, 2, -2, 4)
PATH = {1: 24, -1: 25, 2: 26, -2: 27}
CHUNKS = 28
INNER = ((1, 3), (3, 5), (5, 7), (7, 8))
LEAVES = (
    (1, 1, 7, ((0, 3), (7, 8))),
    (2, -1, 7, ((3, 5), (5, 7))),
    (1, -1, 5, INNER),
    (2, 1, 6, INNER),
    (0, 1, 3, INNER),
    (0, -1, 4, INNER),
)
SIDES = {("z", 1): 0, ("z", -1): 1, ("y", 1): 2, ("y", -1): 3}
CHUNK_US = 1.78
HALF_US = 0.05
HOP_US = 2.8
TABLE_US = 3.0
MARGIN_US = 3.0
KV_ROWS = 40
PARTS = 1
TERMS = 36
NO_TERM = 34
WANT = (1, 2 * RING * RING)


def axis_of(half, major):
    return "zy"[half] if major else "yz"[half]


def ordered(tasks):
    followers = {}
    for task in tasks:
        for dep in task[3]:
            followers.setdefault(dep, []).append(task)
    left = {}

    def remaining(task):
        if task[0] not in left:
            after = max((remaining(t) for t in followers.get(task[0], ())), default=0.0)
            left[task[0]] = task[2] + HOP_US + after
        return left[task[0]]

    arrival, free, result = {}, {}, []
    waiting = list(tasks)
    while waiting:
        best = None
        for task in waiting:
            if all(dep in arrival for dep in task[3]):
                ready = max([arrival[dep] for dep in task[3]], default=0.0)
                key = (max(ready, free.get(task[1], 0.0)), -remaining(task))
                if best is None or key < best[0]:
                    best = (key, task)
        (start, _), task = best
        waiting.remove(task)
        name, link, time, deps = task
        free[link] = start + time
        arrival[name] = start + time + HOP_US
        result.append((start, task))
    return result, arrival


def far_sign(half, row):
    return 1 if (half + row) % 2 == 0 else -1


def gather_tasks():
    tasks = []
    for half in (0, 1):
        minor, major = axis_of(half, False), axis_of(half, True)
        whole = {}
        for step in range(3):
            for sign in (1, -1):
                name = ("H", half, sign, step)
                deps = (("H", half, sign, step - 1),) if step else ()
                tasks.append((name, (major, sign), CHUNK_US, deps))
                if step < 2:
                    whole[PATH[sign * (step + 1)]] = name
                else:
                    whole[8 if sign > 0 else 16] = name
        for row in range(3):
            far = far_sign(half, row)
            for sign in (1, -1):
                for step in range(4 if sign == far else 3):
                    name = ("m", half, row, sign, step)
                    if step:
                        deps = (("m", half, row, sign, step - 1),)
                    else:
                        deps = (whole[8 * row],) if row else ()
                    tasks.append((name, (minor, sign), CHUNK_US, deps))
                    to = 7 if step == 3 else SLOT[sign * (step + 1)]
                    whole[8 * row + to] = name
        for row, sign, to, ranges in LEAVES:
            for lo, hi in ranges:
                deps = tuple(whole[8 * row + s] for s in range(lo, hi) if row or s)
                for r in (0, 1):
                    name = ("L", half, row, sign, to, lo, hi, r)
                    tasks.append((name, (major, sign), CHUNK_US * (hi - lo) / 4, deps))
        copies = tuple(whole.values())
        for sign in (1, -1):
            tasks.append((("G", half, sign), (major, sign), CHUNK_US / 2, copies))
        for sign in (1, -1):
            tasks.append((("X", half, sign), "p", HALF_US, (("G", half, sign),)))
        for row in range(8):
            groups = ((0, 5), (5, 8)) if row < 3 else ((0, 1),) if row < 7 else ()
            for lo, hi in groups:
                if row < 3:
                    deps = tuple(whole[8 * row + s] for s in range(lo, hi) if row or s)
                else:
                    deps = (whole[PATH[ROWS[row]]],)
                tasks.append((("P", half, row, lo, hi), "p", HALF_US * (hi - lo), deps))
    late = [task for _, task in ordered(tasks)[0] if task[0][0] in "PX"]
    main, arrival = ordered([task for task in tasks if task[0][0] not in "PX"])
    result, seen = [], set()
    for start, task in main:
        for other in [t for t in late if t[0][0] == "P"]:
            if set(other[3]) <= seen or max(arrival[d] for d in other[3]) + MARGIN_US < start:
                late.remove(other)
                result.append(other)
                seen.update(other[3])
        result.append(task)
        seen.update(task[3])
    return result + late


def children(row, slot):
    if row == 0:
        return [(3, 1), (4, -1)] if slot else []
    result = []
    if slot:
        result.append((5, -1) if row == 1 else (6, 1))
    if row == 1 and slot in (0, 1, 2, 7):
        result.append((7, 1))
    if row == 2 and slot in (3, 4, 5, 6):
        result.append((7, -1))
    return result


def scatter_tasks():
    tasks = [(("T", 0), "p", TABLE_US, ())]
    for half in (0, 1):
        major = axis_of(half, True)
        for sign in (1, -1):
            tasks.append((("G", half, sign), (major, sign), CHUNK_US / 2, (("T", 0),)))
    leaf = {}
    for row, sign, to, ranges in LEAVES:
        for lo, hi in reversed(ranges):
            for half in (0, 1):
                major = axis_of(half, True)
                for r in (0, 1):
                    name = ("L", half, to, sign, lo, hi, r)
                    deps = (("T", 0),) if r else ()
                    tasks.append((name, (major, -sign), CHUNK_US * (hi - lo) / 4, deps))
                    for s in range(lo, hi):
                        leaf[half, to, s, r] = name
    for half in (0, 1):
        minor, major = axis_of(half, False), axis_of(half, True)
        extra = (("G", half, 1), ("G", half, -1))

        def leaves(row, slot):
            return tuple(leaf[half, to, slot, r] for to, _ in children(row, slot) for r in (0, 1)) + extra

        for row in (1, 2, 0):
            for sign in (1, -1):
                top = 4 if sign == far_sign(half, row) else 3
                for step in range(top, 0, -1):
                    deps = leaves(row, 7 if step == 4 else SLOT[sign * step])
                    if step < top:
                        deps += (("m", half, row, sign, step + 1),)
                    tasks.append((("m", half, row, sign, step), (minor, -sign), CHUNK_US, deps))
        for sign in (1, -1):
            row = 1 if sign > 0 else 2
            for step in (3, 2, 1):
                if step == 3:
                    deps = leaves(row, 0) + (("m", half, row, 1, 1), ("m", half, row, -1, 1))
                else:
                    deps = (("H", half, sign, step + 1),)
                tasks.append((("H", half, sign, step), (major, -sign), CHUNK_US, deps))
        deps = tuple((k, half, s, 1) for k in "H" for s in (1, -1))
        deps += (("m", half, 0, 1, 1), ("m", half, 0, -1, 1))
        tasks.append((("F", half), ("f", half), 0.0, deps))
    return [task for _, task in ordered(tasks)[0]]


GATHER = gather_tasks()
SCATTER = scatter_tasks()
GATHER_SENDS = {task[0]: i for i, task in enumerate(GATHER)}
SCATTER_SENDS = {t[0]: i for i, t in enumerate(t for t in SCATTER if t[0][0] != "F")}


def place():
    seq = lax.axis_index("seq")
    head = lax.axis_index("head")
    return seq, head, seq // 16, (seq // 2) % RING, seq % 2


def neighbours(seq, head, z, y, core):
    up = lambda v: lax.rem(v + 1, RING)
    down = lambda v: lax.rem(v + RING - 1, RING)
    index = lambda zz, yy, cc: zz * 16 + yy * 2 + cc
    count = 2 * RING * RING
    peers = {}
    for name, cc in ((0, core), (1, 1 - core)):
        peers["z", 1, name] = index(up(z), y, cc)
        peers["z", -1, name] = index(down(z), y, cc)
        peers["y", 1, name] = index(z, up(y), cc)
        peers["y", -1, name] = index(z, down(y), cc)
    peers["p"] = index(z, y, 1 - core)
    peers["next"] = lax.rem(seq + 1, count)
    peers["last"] = lax.rem(seq + count - 1, count)
    return {k: {"seq": v, "head": head} for k, v in peers.items()}


def enter(peers, seq, head):
    barrier = pltpu.get_barrier_semaphore()
    everyone = list(peers.values())
    everyone += [{"seq": seq, "head": lax.rem(head + j, KVH)} for j in (1, 2, 3)]
    for peer in everyone:
        pl.semaphore_signal(barrier, inc=1, device_id=peer, device_id_type=MESH)
    pl.semaphore_wait(barrier, len(everyone))


def remote(src, dst, send, recv, peer):
    return pltpu.make_async_remote_copy(
        src_ref=src,
        dst_ref=dst,
        send_sem=send,
        recv_sem=recv,
        device_id=peer,
        device_id_type=MESH,
    )


def owner_of(half, z, y, core, far, near):
    dz, dy = (far, near) if half == 0 else (near, far)
    return lax.rem(z - dz + RING, RING) * 16 + lax.rem(y - dy + RING, RING) * 2 + core


def chunk_offsets(chunk):
    if chunk < 24:
        return ROWS[chunk // 8], ORDER[chunk % 8]
    return (1, -1, 2, -2)[chunk - 24], 0


def chosen(value, table):
    result = table[0]
    for i, entry in enumerate(table[1:], 1):
        result = jnp.where(value == i, entry, result)
    return result


SLOTS_MOD = [SLOT[d] if d <= 4 else SLOT[d - RING] for d in range(RING)]
ROWS_MOD = [ROWS.index(d) if d <= 4 else ROWS.index(d - RING) for d in range(RING)]
SLOTS_PACKED = sum(v << (3 * d) for d, v in enumerate(SLOTS_MOD))
ROWS_PACKED = sum(v << (3 * d) for d, v in enumerate(ROWS_MOD))
PARENT = [0, 0, 0, 2, 1, 1, 2, 2]


def relation(z, y, owner, half):
    dz = (z + RING - owner // 16) % RING
    dy = (y + RING - (owner // 2) % RING) % RING
    far, near = (dz, dy) if half == 0 else (dy, dz)
    return chosen(far, ROWS_MOD), chosen(near, SLOTS_MOD)


def gather_kernel(
    keys, values, rand, glob, sel_out, near_out, cand_out, wants, want,
    full0, full1, picked, staged, extra, scal, send, recv, xsend, xrecv, osend, orecv, lsem, csem,
):
    seq, head, z, y, core = place()
    peers = neighbours(seq, head, z, y, core)
    full = (full0, full1)
    lane = lax.broadcasted_iota(jnp.int32, (1, 2 * RING * RING), 1)
    named = jnp.full_like(lane, 4 * NO_TERM)
    for e in range(4 * RAND):
        block = rand[e // RAND, e % RAND]
        named = jnp.where(lane == block // 4, 4 * e + block % 4, named)
    want[...] = named
    local = pltpu.make_async_copy(want, wants.at[8], lsem.at[0])
    local.start()
    local.wait()
    enter(peers, seq, head)
    pieces = (keys, values)
    xcopies = []
    for j in (1, 2, 3):
        to = lax.rem(head + j, KVH)
        for n, source in enumerate(pieces):
            xcopies.append(
                remote(
                    source.at[:, pl.ds(pl.multiple_of(to * DH, DH), DH)],
                    full[n].at[0, head],
                    xsend.at[j - 1, n],
                    xrecv.at[j - 1, n],
                    {"seq": seq, "head": to},
                )
            )
            xcopies[-1].start()
    ocopies = [remote(wants.at[8], wants.at[9], osend.at[0], orecv.at[0], peers["p"])]
    for (axis, sign), side in SIDES.items():
        back = SIDES[axis, -sign] * 2
        for r in (0, 1):
            i = len(ocopies)
            peer = peers[axis, sign, r]
            ocopies.append(remote(wants.at[8], wants.at[back + r], osend.at[i], orecv.at[i], peer))
    for copy in ocopies:
        copy.start()
    local = []
    for n, source in enumerate(pieces):
        mine = source.at[:, pl.ds(pl.multiple_of(head * DH, DH), DH)]
        local.append(pltpu.make_async_copy(mine, full[n].at[0, head], lsem.at[1 + n]))
    for copy in local:
        copy.start()
    for copy in local:
        copy.wait()
    for copy in xcopies:
        copy.wait_recv()

    started = {}
    waited = set()
    tail = []

    def wait_for(deps):
        for dep in deps:
            if dep not in waited:
                waited.add(dep)
                started[dep].wait_recv()

    def finish_start():
        for copy in ocopies:
            copy.wait_recv()
        scalars = pltpu.make_async_copy(wants, scal, lsem.at[0])
        scalars.start()
        for half in (0, 1):
            i = 10 + 2 * half
            tail.append(remote(full[half].at[0, 3], near_out.at[half, 0], osend.at[i], orecv.at[i], peers["next"]))
            tail.append(
                remote(full[half].at[0, 0], near_out.at[half, 5], osend.at[i + 1], orecv.at[i + 1], peers["last"])
            )
            tail.append(
                pltpu.make_async_copy(full[half].at[0], near_out.at[half, pl.ds(1, 4)], lsem.at[1 + half])
            )
        for copy in tail:
            copy.start()
        scalars.wait()

    def pick(half, chunk, side):
        far, near = chunk_offsets(chunk)
        inner = scal[side, 0, owner_of(half, z, y, core, far, near)] % 4
        block = full[half][chunk, 0]
        for b in (1, 2, 3):
            block = jnp.where(inner == b, full[half][chunk, b], block)
        return block

    ready = False
    passed = set()
    locals_ = []
    for name, link, _, deps in GATHER:
        wait_for(deps)
        kind, half = name[:2]
        major = axis_of(half, True)
        if kind in "LP" and not ready:
            finish_start()
            ready = True
        i = GATHER_SENDS[name]
        peer = peers["p"] if link == "p" else peers[link[0], link[1], 0]
        extra_sends = []
        if kind == "H":
            _, _, sign, step = name
            src = full[half].at[PATH[sign * step] if step else 0]
            dst = full[half].at[PATH[sign * (step + 1)] if step < 2 else (8 if sign > 0 else 16)]
        elif kind == "m":
            _, _, row, sign, step = name
            src = full[half].at[8 * row + SLOT[sign * step]]
            dst = full[half].at[8 * row + (7 if step == 3 else SLOT[sign * (step + 1)])]
        elif kind == "L":
            _, _, row, sign, to, lo, hi, r = name
            side = SIDES[major, sign] * 2
            for s in range(lo, hi):
                staged[half, r, to, s] = pick(half, 8 * row + s, side + r)
            src = staged.at[half, r, to, pl.ds(lo, hi - lo)]
            dst = sel_out.at[r, half, to, pl.ds(lo, hi - lo)]
            peer = peers[major, sign, r]
        elif kind == "P":
            _, _, row, lo, hi = name
            for s in range(lo, hi):
                chunk = 8 * row + s if row < 3 else PATH[ROWS[row]] if row < 7 and s == 0 else None
                if chunk is not None:
                    for r in (0, 1):
                        picked[half, r, row, s] = pick(half, chunk, 8 + r)
            span = pl.ds(lo, hi - lo)
            src = picked.at[half, 1, row, span]
            dst = sel_out.at[1, half, row, span]
            keep = pltpu.make_async_copy(
                picked.at[half, 0, row, span], sel_out.at[0, half, row, span], csem.at[len(locals_)]
            )
            keep.start()
            locals_.append(keep)
        elif kind == "G":
            sign = name[2]
            if half not in passed:
                passed.add(half)
                for k in (0, 1):
                    row, slot = relation(z, y, glob[k] // 4, half)
                    chunk = jnp.where(row < 3, row * 8 + slot, jnp.where(row < 7, 21 + row, 0))
                    extra[half, k] = full[half][chunk, glob[k] % 4]
                keep = pltpu.make_async_copy(extra.at[half], cand_out.at[0, half, 0], csem.at[len(locals_)])
                keep.start()
                locals_.append(keep)
                j = 14 + half
                tail.append(
                    remote(extra.at[half], cand_out.at[1, half, 0], osend.at[j], orecv.at[j], peers["p"])
                )
                tail[-1].start()
            src = extra.at[half]
            dst = cand_out.at[0, half, 2 if sign > 0 else 1]
        else:
            sign = name[2]
            at = 2 if sign > 0 else 1
            src = cand_out.at[0, half, at]
            dst = cand_out.at[1, half, at]
        copy = remote(src, dst, send.at[i], recv.at[i], peer)
        copy.start()
        started[name] = copy
    wait_for(started)
    for copy in xcopies + ocopies + list(started.values()):
        copy.wait_send()
    for copy in tail + locals_:
        copy.wait()


def gather_all(keys, values, rand, glob):
    count = len(GATHER)
    keeps = 2 + sum(task[0][0] == "P" for task in GATHER)
    hbm = pl.BlockSpec(memory_space=pl.ANY)
    vmem = pl.BlockSpec(memory_space=pltpu.VMEM)
    smem = pl.BlockSpec(memory_space=pltpu.SMEM)
    return pl.pallas_call(
        gather_kernel,
        out_shape=(
            jax.ShapeDtypeStruct((2, 2, 8, 8, BLOCK, DH), BF16),
            jax.ShapeDtypeStruct((2, 6, BLOCK, DH), BF16),
            jax.ShapeDtypeStruct((2, 2, 3, 2, BLOCK, DH), BF16),
            jax.ShapeDtypeStruct((10,) + WANT, jnp.int32),
        ),
        in_specs=[vmem] * 2 + [smem] * 2,
        out_specs=(hbm, hbm, hbm, vmem),
        scratch_shapes=[
            pltpu.VMEM(WANT, jnp.int32),
            pltpu.VMEM((CHUNKS, 4, BLOCK, DH), BF16),
            pltpu.VMEM((CHUNKS, 4, BLOCK, DH), BF16),
            pltpu.VMEM((2, 2, 8, 8, BLOCK, DH), BF16),
            pltpu.VMEM((2, 2, 8, 8, BLOCK, DH), BF16),
            pltpu.VMEM((2, 2, BLOCK, DH), BF16),
            pltpu.SMEM((10,) + WANT, jnp.int32),
            pltpu.SemaphoreType.DMA((count,)),
            pltpu.SemaphoreType.DMA((count,)),
            pltpu.SemaphoreType.DMA((3, 2)),
            pltpu.SemaphoreType.DMA((3, 2)),
            pltpu.SemaphoreType.DMA((16,)),
            pltpu.SemaphoreType.DMA((16,)),
            pltpu.SemaphoreType.DMA((3,)),
            pltpu.SemaphoreType.DMA((keeps,)),
        ],
        compiler_params=pltpu.CompilerParams(collective_id=1, has_side_effects=True),
        name="gather_blocks",
    )(keys, values, rand, glob)


def scatter_kernel(
    wants, glob, table, own, halo, dk, dv,
    mirror, staged, landed, line, origin, path, stem, gsum, gin, extra, rim, final,
    send, recv, xsend, xrecv, hsem, lsem,
):
    seq, head, z, y, core = place()
    peers = neighbours(seq, head, z, y, core)
    enter(peers, seq, head)
    first = []
    for half in (0, 1):
        i = 2 * half
        first.append(remote(halo.at[half, 0], rim.at[half, 1], hsem.at[0, i], hsem.at[1, i], peers["last"]))
        first.append(
            remote(halo.at[half, 1], rim.at[half, 0], hsem.at[0, i + 1], hsem.at[1, i + 1], peers["next"])
        )
    started = {}
    waited = set()
    ready = set()
    passed = set()

    def block_sum(half, chunk, sides, b):
        far, near = chunk_offsets(chunk)
        owner = owner_of(half, z, y, core, far, near)
        mine, theirs = wants[8, 0, owner], wants[9, 0, owner]
        total = jnp.where(mine % 4 == b, table[half, mine // 4].astype(F32), 0.0)
        total += jnp.where(theirs % 4 == b, mirror[half, theirs // 4].astype(F32), 0.0)
        kind = sum(1 if sign > 0 else 2 for _, sign in sides)
        number = owner * 4 + b
        total += jnp.where(
            number == glob[0],
            extra[half, kind, 0],
            jnp.where(number == glob[1], extra[half, kind, 1], 0.0),
        )
        major = axis_of(half, True)
        for to, sign in sides:
            for r in (0, 1):
                inner = wants[SIDES[major, sign] * 2 + r, 0, owner] % 4
                term = landed[half, r, to, chunk % 8].astype(F32)
                total += jnp.where(inner == b, term, 0.0)
        return total

    for name, link, _, deps in SCATTER:
        for dep in deps:
            if dep not in waited:
                waited.add(dep)
                started[dep].wait_recv()
        kind, half = name[:2]
        if kind in "mHF" and half not in ready:
            ready.add(half)
            for k in (0, 1):
                alone = table[half, 32 + k].astype(F32) + mirror[half, 32 + k].astype(F32)
                up, down = gin[half, 0, k].astype(F32), gin[half, 1, k].astype(F32)
                extra[half, 0, k] = alone
                extra[half, 1, k] = alone + up
                extra[half, 2, k] = alone + down
                extra[half, 3, k] = alone + up + down
        if kind == "F":
            for copy in first[2 * half : 2 * half + 2]:
                copy.wait_recv()

            for b in range(4):
                total = block_sum(half, 0, [], b) + own[half, b]
                total += line[half, 0, 0, b].astype(F32) + origin[half, 0, b].astype(F32)
                total += stem[half, 0, b].astype(F32) + stem[half, 1, b].astype(F32)
                if b in (0, 3):
                    total += rim[half, b // 3].astype(F32)
                final[half, b] = total.astype(BF16)
            continue
        if kind == "T":
            src, dst = table, mirror
        elif kind == "G":
            if half not in passed:
                passed.add(half)
                for k in (0, 1):
                    alone = table[half, 32 + k].astype(F32) + mirror[half, 32 + k].astype(F32)
                    gsum[half, k] = alone.astype(BF16)
            src, dst = gsum.at[half], gin.at[half, 1 if name[2] > 0 else 0]
        elif kind == "L":
            _, _, to, sign, lo, hi, r = name
            for s in range(lo, hi):
                owner = owner_of(half, z, y, core, ROWS[to], ORDER[s])
                staged[half, r, to, s] = (table, mirror)[r][half, wants[8 + r, 0, owner] // 4]
            span = pl.ds(lo, hi - lo)
            src, dst = staged.at[half, r, to, span], landed.at[half, r, to, span]
        elif kind == "m":
            _, _, row, sign, step = name
            slot = 7 if step == 4 else SLOT[sign * step]
            arrived = any(dep[0] == "m" for dep in deps)
            sides = children(row, slot)

            @pl.loop(0, 4)
            def _(b):
                total = block_sum(half, 8 * row + slot, sides, b)
                if arrived:
                    total += line[half, row, slot, b].astype(F32)
                line[half, row, slot, b] = total.astype(BF16)

            src = line.at[half, row, slot]
            if step > 1:
                dst = line.at[half, row, SLOT[sign * (step - 1)]]
            else:
                dst = line.at[half, row, 0] if sign > 0 else origin.at[half, row]
        else:
            _, _, sign, step = name
            if step == 3:
                row = 1 if sign > 0 else 2
                sides = children(row, 0)

                @pl.loop(0, 4)
                def _(b):
                    total = block_sum(half, 8 * row, sides, b)
                    total += line[half, row, 0, b].astype(F32) + origin[half, row, b].astype(F32)
                    line[half, row, 0, b] = total.astype(BF16)

                src = line.at[half, row, 0]
            else:
                chunk = PATH[sign * step]

                @pl.loop(0, 4)
                def _(b):
                    total = block_sum(half, chunk, [], b) + path[half, chunk - 24, b].astype(F32)
                    path[half, chunk - 24, b] = total.astype(BF16)

                src = path.at[half, chunk - 24]
            if step > 1:
                dst = path.at[half, PATH[sign * (step - 1)] - 24]
            else:
                dst = stem.at[half, 0 if sign > 0 else 1]
        i = SCATTER_SENDS[name]
        peer = peers["p"] if link == "p" else peers[link[0], link[1], 0]
        copy = remote(src, dst, send.at[i], recv.at[i], peer)
        copy.start()
        started[name] = copy
        if kind == "T":
            for copy in first:
                copy.start()

    here = pl.ds(pl.multiple_of(head * DH, DH), DH)
    copies = []
    for j in (1, 2, 3):
        to = lax.rem(head + j, KVH)
        for n, target in enumerate((dk, dv)):
            copies.append(
                remote(
                    final.at[n, to],
                    target.at[:, here],
                    xsend.at[j - 1, n],
                    xrecv.at[j - 1, n],
                    {"seq": seq, "head": to},
                )
            )
            copies[-1].start()
    for n, target in enumerate((dk, dv)):
        copies.append(pltpu.make_async_copy(final.at[n, head], target.at[:, here], lsem.at[n]))
        copies[-1].start()
    for copy in copies:
        copy.wait()
    for copy in first + list(started.values()):
        copy.wait_send()


def scatter_all(wants, glob, table, own, halo):
    count = len(SCATTER_SENDS)
    vmem = pl.BlockSpec(memory_space=pltpu.VMEM)
    smem = pl.BlockSpec(memory_space=pltpu.SMEM)
    tile = (BLOCK, DH)
    return pl.pallas_call(
        scatter_kernel,
        out_shape=(jax.ShapeDtypeStruct((BLOCK, KVH * DH), BF16),) * 2,
        in_specs=[smem] * 2 + [vmem] * 3,
        out_specs=(pl.BlockSpec(memory_space=pl.ANY),) * 2,
        scratch_shapes=[
            pltpu.VMEM((2, TERMS) + tile, BF16),
            pltpu.VMEM((2, 2, 8, 8) + tile, BF16),
            pltpu.VMEM((2, 2, 8, 8) + tile, BF16),
            pltpu.VMEM((2, 3, 8, 4) + tile, BF16),
            pltpu.VMEM((2, 3, 4) + tile, BF16),
            pltpu.VMEM((2, 4, 4) + tile, BF16),
            pltpu.VMEM((2, 2, 4) + tile, BF16),
            pltpu.VMEM((2, 2) + tile, BF16),
            pltpu.VMEM((2, 2, 2) + tile, BF16),
            pltpu.VMEM((2, 4, 2) + tile, F32),
            pltpu.VMEM((2, 2) + tile, BF16),
            pltpu.VMEM((2, 4) + tile, BF16),
            pltpu.SemaphoreType.DMA((count,)),
            pltpu.SemaphoreType.DMA((count,)),
            pltpu.SemaphoreType.DMA((3, 2)),
            pltpu.SemaphoreType.DMA((3, 2)),
            pltpu.SemaphoreType.DMA((2, 4)),
            pltpu.SemaphoreType.DMA((2,)),
        ],
        compiler_params=pltpu.CompilerParams(collective_id=2, has_side_effects=True),
        name="scatter_terms",
    )(wants, glob, table, own, halo)


def attention_kernel(
    rand, ids, queries, d_out, selected, nearby, candidates,
    out, dq, table, own, halo, kv, near, glob, sems, gsems,
):
    seq, _, z, y, core = place()
    copies = [pltpu.make_async_copy(nearby.at[n], kv.at[n, pl.ds(0, 6)], gsems.at[n]) for n in (0, 1)]
    for copy in copies:
        copy.start()

    def fetch(n, e, spot):
        return pltpu.make_async_copy(selected.at[spot], kv.at[n, 8 + e], sems.at[n, e])

    for k in (0, 1):
        owner = ids[k] // 4
        away = (owner + core) % 2
        for n in (0, 1):
            row, slot = relation(z, y, owner, n)
            whole = (row < 3) | ((slot == 0) & (row < 7))
            parent = chosen(row, PARENT)
            parent = jnp.where((row == 7) & (slot >= 3) & (slot < 7), 1, parent)
            parent = jnp.where(whole, 0, parent)
            spot = ((away * 2 + n) * 3 + parent) * 2 + k
            copies.append(
                pltpu.make_async_copy(candidates.at[spot], kv.at[n, 6 + k], gsems.at[2 + 2 * n + k])
            )
            copies[-1].start()
    def start_fetches(i, e):
        owner = rand[i, e] // 4
        away = (owner + core) % 2
        dz = 3 * ((z + RING - owner // 16) % RING)
        dy = 3 * ((y + RING - (owner // 2) % RING) % RING)
        for n, far, near_by in ((0, dz, dy), (1, dy, dz)):
            at = ((ROWS_PACKED >> far) & 7) * 8 + ((SLOTS_PACKED >> near_by) & 7)
            fetch(n, i * RAND + e, (away * 2 + n) * 64 + at).start()

    for e in range(RAND):
        start_fetches(0, e)
    near[...] = jnp.zeros_like(near)
    glob[...] = jnp.zeros_like(glob)
    for n in (0, 1):
        table[n, NO_TERM:] = jnp.zeros((TERMS - NO_TERM, BLOCK, DH), BF16)
    for copy in copies:
        copy.wait()
    factor = DH ** (-0.5)
    dims = lambda a, b: (((a,), (b,)), ((), ()))

    def dot(a, b, at, bt):
        return lax.dot_general(a, b, dims(at, bt), preferred_element_type=F32)

    for i in range(4):
        for e in range(RAND):
            for n in (0, 1):
                fetch(n, i * RAND + e, 0).wait()
            if i < 3:
                start_fetches(i + 1, e)
        rows = pl.ds(i * BLOCK, BLOCK)
        def listed(n):
            return jnp.concatenate(
                [
                    kv[n, pl.ds(i, 3)].reshape(3 * BLOCK, DH),
                    kv[n, 6:8].reshape(2 * BLOCK, DH),
                    kv[n, pl.ds(8 + i * RAND, RAND)].reshape(RAND * BLOCK, DH),
                ],
                axis=0,
            )

        k, v = listed(0), listed(1)
        cut_first = jnp.logical_and(i == 0, seq == 0)
        cut_last = jnp.logical_and(i == 3, seq == lax.axis_size("seq") - 1)
        sums = [None, None]
        for part in range(PARTS):
            heads = range(part * HEADS // PARTS, (part + 1) * HEADS // PARTS)
            stack = lambda ref: jnp.concatenate([ref[rows, h * DH : (h + 1) * DH] for h in heads], axis=0)
            q, g = stack(queries), stack(d_out)
            scores = dot(k, q, 1, 1) * factor
            scores = jnp.concatenate(
                [
                    jnp.where(cut_first, NEG_FILL, scores[:BLOCK]),
                    scores[BLOCK : 2 * BLOCK],
                    jnp.where(cut_last, NEG_FILL, scores[2 * BLOCK : 3 * BLOCK]),
                    scores[3 * BLOCK :],
                ],
                axis=0,
            )
            peak = jnp.max(scores, axis=0, keepdims=True)
            weights = jnp.exp(scores - peak)
            probs = weights * (1.0 / jnp.sum(weights, axis=0, keepdims=True))
            probs16 = probs.astype(BF16)
            result = dot(v, probs16, 0, 0).astype(BF16)
            delta = jnp.sum(g.T.astype(F32) * result.astype(F32), axis=0, keepdims=True)
            dprobs = dot(v, g, 1, 1)
            dscores = (probs * (dprobs - delta)).astype(BF16)
            dquery = (dot(k, dscores, 0, 0) * factor).astype(BF16).T
            result = result.T
            for n, h in enumerate(heads):
                out[rows, h * DH : (h + 1) * DH] = result[n * BLOCK : (n + 1) * BLOCK]
                dq[rows, h * DH : (h + 1) * DH] = dquery[n * BLOCK : (n + 1) * BLOCK]
            for n, terms in ((0, dot(dscores, q, 1, 0)), (1, dot(probs16, g, 1, 0))):
                sums[n] = terms if sums[n] is None else sums[n] + terms
        for n, terms in ((0, sums[0] * factor), (1, sums[1])):
            near[n, pl.ds(i, 3)] += terms[: 3 * BLOCK].reshape(3, BLOCK, DH)
            glob[n] += terms[3 * BLOCK : 5 * BLOCK].reshape(2, BLOCK, DH)
            table[n, pl.ds(i * RAND, RAND)] = terms[5 * BLOCK :].astype(BF16).reshape(RAND, BLOCK, DH)

    for n in (0, 1):
        own[n] = near[n, 1:5]
        halo[n, 0] = near[n, 0].astype(BF16)
        halo[n, 1] = near[n, 5].astype(BF16)
        for a in (0, 1):
            total = glob[n, a] + jnp.where(ids[0] == ids[1], glob[n, 1 - a], 0.0)
            table[n, 32 + a] = total.astype(BF16)


def attention(rand, ids, queries, d_out, selected, nearby, candidates):
    smem = pl.BlockSpec(memory_space=pltpu.SMEM)
    vmem = pl.BlockSpec(memory_space=pltpu.VMEM)
    tile = (BLOCK, DH)
    return pl.pallas_call(
        attention_kernel,
        out_shape=(
            jax.ShapeDtypeStruct(queries.shape, BF16),
            jax.ShapeDtypeStruct(queries.shape, BF16),
            jax.ShapeDtypeStruct((2, TERMS) + tile, BF16),
            jax.ShapeDtypeStruct((2, 4) + tile, F32),
            jax.ShapeDtypeStruct((2, 2) + tile, BF16),
        ),
        in_specs=[smem] * 2 + [vmem] * 2 + [pl.BlockSpec(memory_space=pl.ANY)] * 3,
        out_specs=(vmem,) * 5,
        scratch_shapes=[
            pltpu.VMEM((2, KV_ROWS) + tile, BF16),
            pltpu.VMEM((2, 6) + tile, F32),
            pltpu.VMEM((2, 2) + tile, F32),
            pltpu.SemaphoreType.DMA((2, 4 * RAND)),
            pltpu.SemaphoreType.DMA((6,)),
        ],
        compiler_params=pltpu.CompilerParams(vmem_limit_bytes=60 * 1024 * 1024),
        name="block_attention",
    )(rand, ids, queries, d_out, selected, nearby, candidates)


def copy_kernel(a, b, x, y):
    x[...] = a[...]
    y[...] = b[...]


def body(queries, keys, values, d_out, rand_blocks, glob_blocks):
    selected, nearby, candidates, wants = gather_all(keys, values, rand_blocks, glob_blocks)
    out, dq, table, own, halo = attention(
        rand_blocks,
        glob_blocks,
        queries,
        d_out,
        selected.reshape(256, BLOCK, DH),
        nearby,
        candidates.reshape(24, BLOCK, DH),
    )
    dk, dv = scatter_all(wants, glob_blocks, table, own, halo)
    dk, dv = pl.pallas_call(
        copy_kernel, out_shape=[jax.ShapeDtypeStruct(dk.shape, dk.dtype)] * 2, name="write_out"
    )(dk, dv)
    return (out, dq, dk, dv)


def solution(mesh):
    in_specs = (
        P("seq", "head"),
        P(("seq", "head"), None),
        P(("seq", "head"), None),
        P("seq", "head"),
        P("seq", None),
        P(),
    )
    out_specs = (
        P("seq", "head"),
        P("seq", "head"),
        P(("seq", "head"), None),
        P(("seq", "head"), None),
    )
    return jax.shard_map(body, mesh=mesh, in_specs=in_specs, out_specs=out_specs, check_vma=False)
```
